128 devices in a mesh: gx: 8 (over x, y_lo), gy: 16 (over z, y_hi, core).
Axes of the slice: x: 4, y: 4 (y_hi: 2, y_lo: 2; y = y_hi * 2 + y_lo), z: 4, core: 2. Of those that a mesh axis runs over, the one named last changes fastest.
Arguments:
- xi_coarse: float32 [1024, 2048], P('gx', 'gy'), may hold values from -6 to 6
- xi_middle: float32 [2048, 4096], P('gx', 'gy'), may hold values from -6 to 6
- xi_fine: float32 [4096, 8192], P('gx', 'gy'), may hold values from -6 to 6
- coef_middle: bfloat16 [4, 9, 1024, 2048], P(None, None, 'gx', 'gy'), may hold values from -1.1953125 to 1.1953125
- coef_fine: bfloat16 [4, 9, 2048, 4096], P(None, None, 'gx', 'gy'), may hold values from -1.1953125 to 1.1953125
- kern_u: bfloat16 [8, 32, 1024, 512], P('gx', 'gy'), may hold values from -0.25 to 0.25
- kern_v: bfloat16 [8, 32, 1024, 512], P('gx', 'gy'), may hold values from -0.25 to 0.25
- vis_data: bfloat16 [8, 32, 1024, 1024], P('gx', 'gy'), may hold values from -6 to 6
- facet_tiles: int32 [8, 32, 2], P('gx', 'gy'), may hold values from 0 to 15, as said below
- facet_weight: float32 [8, 32, 2], P('gx', 'gy'), may hold values from 0.5 to 1.5
- facet_count: int32 [8, 32], P('gx', 'gy'), may hold values from 256 to 1024, as said below
Outputs:
- grad_coarse: float32 [1024, 2048], P('gx', 'gy')
- grad_middle: float32 [2048, 4096], P('gx', 'gy')
- grad_fine: float32 [4096, 8192], P('gx', 'gy')
- potential: float32 [], replicated
The draws below stay inside these ranges and needn't reach their ends.
Inputs may be any that keep to these rules, and one draw needn't show every extreme that they name: `facet_tiles`: every tile column of a row is named by some facet of that row. `facet_count`: bins 0 to the count minus one of a facet are used.
All inputs are finite; a program needn't handle non-finite values.
Results may differ from the reference program's by a relative error of at most 0.0085.
Values may be sent and summed in bfloat16 or wider, within the bound.
A program may use at most 320 MiB of HBM per device.

```python
import jax
import jax.numpy as jnp
from jax import lax

TS = 512
BINS = 1024
FAC_DEV = 2
LIST = 2
TROW = 16
FROWS = 8
FCOLS = 32
NC0R = 1024
NC0C = 2048
NC1R = 2048
NC1C = 4096
NC2R = 4096
NC2C = 8192


def draw_facet_tiles(key, part):
    keys = jax.random.split(key, FROWS + 1)
    leading = jax.vmap(lambda one_key: jax.random.permutation(one_key, TROW))(keys[:FROWS]).astype(jnp.int32)
    others = jax.random.randint(keys[FROWS], (FROWS, FCOLS, LIST), 0, TROW).astype(jnp.int32)
    spread = jnp.repeat(leading, FAC_DEV, axis=1)
    first_kind = (jnp.arange(FCOLS, dtype=jnp.int32) % FAC_DEV == 0)[None, :]
    first_slot = jnp.where(first_kind, spread, others[:, :, 0])
    return others.at[:, :, 0].set(first_slot)


def draw_facet_count(key, part):
    counts = jax.random.randint(key, (FROWS, FCOLS), BINS // 4, BINS + 1).astype(jnp.int32)
    counts = counts.at[0, 0].set(BINS)
    return counts.at[0, 1].set(BINS // 4)


def block_scale(rng, extent, shards, smallest, high):
    level = 1.0
    for dim, blocks in shards:
        steps = jax.random.uniform(jax.random.fold_in(jax.random.fold_in(rng, 6), dim), (blocks,), jnp.float32, smallest / len(shards), high / len(shards))
        level = level * jnp.repeat(jnp.exp(steps), extent[dim] // blocks).reshape((-1,) + (1,) * (len(extent) - 1 - dim))
    return level


def bell_draw(own_key, extent, scale, limit, cuts=(), held_as=jnp.bfloat16):
    level = block_scale(own_key, extent, cuts, -0.22, 0.18) if cuts else 1.0
    drawn = jax.random.normal(own_key, extent, jnp.float32) * scale * level
    return jnp.minimum(jnp.maximum(drawn, -limit), limit).astype(held_as)


def setup_inputs(seed: int = 0) -> dict:
    key_list = jax.random.split(jax.random.key(seed), 12)
    xi_coarse = bell_draw(key_list[0], (NC0R, NC0C), 1.0, 6.0, ((0, 8), (1, 16)), jnp.float32)
    xi_middle = bell_draw(key_list[1], (NC1R, NC1C), 1.0, 6.0, ((0, 8), (1, 16)), jnp.float32)
    xi_fine = bell_draw(key_list[2], (NC2R, NC2C), 1.0, 6.0, ((0, 8), (1, 16)), jnp.float32)
    coef_middle = bell_draw(key_list[3], (4, 9, NC0R, NC0C), 0.2, 1.1953125, ((2, 8), (3, 16)))
    coef_fine = bell_draw(key_list[4], (4, 9, NC1R, NC1C), 0.2, 1.1953125, ((2, 8), (3, 16)))
    kern_u = bell_draw(key_list[5], (FROWS, FCOLS, BINS, TS), TS ** -0.5, 0.25, ((0, 8), (1, 16)))
    kern_v = bell_draw(key_list[6], (FROWS, FCOLS, BINS, TS), TS ** -0.5, 0.25, ((0, 8), (1, 16)))
    vis_data = bell_draw(key_list[7], (FROWS, FCOLS, BINS, BINS), 1.0, 6.0, ((0, 8), (1, 16)))
    facet_tiles = draw_facet_tiles(jax.random.fold_in(key_list[11], 71), 0)
    facet_weight = jnp.clip(0.5 + 1.0 * jax.random.uniform(key_list[9], (FROWS, FCOLS, LIST), jnp.float32) ** block_scale(key_list[9], (FROWS, FCOLS, LIST), ((0, 8), (1, 16)), -0.2, 0.2), 0.5, 1.5)
    facet_count = draw_facet_count(jax.random.fold_in(key_list[11], 71), 0)
    return dict(xi_coarse=xi_coarse, xi_middle=xi_middle, xi_fine=xi_fine, coef_middle=coef_middle, coef_fine=coef_fine, kern_u=kern_u, kern_v=kern_v, vis_data=vis_data, facet_tiles=facet_tiles, facet_weight=facet_weight, facet_count=facet_count)


inv_noise = 0.125


def alternate(quads, rows, cols):
    return quads.reshape(2, 2, rows, cols).transpose(2, 0, 3, 1).reshape(2 * rows, 2 * cols)


def refine(padded, weights):
    rows, cols = weights.shape[2], weights.shape[3]
    quads = []
    for child in range(4):
        total = jnp.zeros((rows, cols), jnp.float32)
        for near in range(9):
            shift_r, shift_c = near // 3 - 1, near % 3 - 1
            window = padded[1 + shift_r:1 + shift_r + rows, 1 + shift_c:1 + shift_c + cols]
            total = total + weights[child, near].astype(jnp.float32) * window
        quads.append(total)
    return alternate(jnp.stack(quads), rows, cols)


def parent_terms(grad, weights):
    rows, cols = weights.shape[2], weights.shape[3]
    quads = grad.reshape(rows, 2, cols, 2).transpose(1, 3, 0, 2).reshape(4, rows, cols)
    parts = []
    for near in range(9):
        total = jnp.zeros((rows, cols), jnp.float32)
        for child in range(4):
            total = total + weights[child, near].astype(jnp.float32) * quads[child]
        parts.append(total)
    return jnp.stack(parts)


def collect_back(padded, rows, cols):
    total = jnp.zeros((rows, cols), jnp.float32)
    for near in range(9):
        shift_r, shift_c = near // 3 - 1, near % 3 - 1
        total = total + padded[near, 1 - shift_r:1 - shift_r + rows, 1 - shift_c:1 - shift_c + cols]
    return total


def back(grad, weights):
    rows, cols = weights.shape[2], weights.shape[3]
    stack = parent_terms(grad, weights)
    return collect_back(jnp.pad(stack, ((0, 0), (1, 1), (1, 1))), rows, cols)


def one_facet(items):
    fsum, ku, kv, data, count = items
    amp = jnp.dot(ku, fsum.astype(jnp.bfloat16), preferred_element_type=jnp.float32).astype(jnp.bfloat16)
    vis = jnp.dot(amp, kv.T, preferred_element_type=jnp.float32)
    live = (jnp.arange(BINS, dtype=jnp.int32) < count).astype(jnp.float32)
    resid = live[:, None] * (vis - data.astype(jnp.float32))
    lik = 0.5 * inv_noise * jnp.sum(resid * resid)
    dvis = (inv_noise * resid).astype(jnp.bfloat16)
    damp = jnp.dot(dvis, kv, preferred_element_type=jnp.float32).astype(jnp.bfloat16)
    dsum = jnp.dot(ku.T, damp, preferred_element_type=jnp.float32)
    return lik, dsum


def reference(xi_coarse, xi_middle, xi_fine, coef_middle, coef_fine, kern_u, kern_v, vis_data, facet_tiles, facet_weight, facet_count):
    level_middle = refine(jnp.pad(xi_coarse, 1), coef_middle) + xi_middle
    level_fine = refine(jnp.pad(level_middle, 1), coef_fine) + xi_fine
    sky = level_fine.astype(jnp.bfloat16)
    tiles = sky.reshape(FROWS, TS, TROW, TS).transpose(0, 2, 1, 3).astype(jnp.float32)
    onehot = (facet_tiles[:, :, :, None] == jnp.arange(TROW, dtype=jnp.int32)).astype(jnp.float32)
    mixing = jnp.sum(facet_weight[:, :, :, None] * onehot, axis=2)
    sums = jnp.einsum("rqt,rtxy->rqxy", mixing, tiles, precision=lax.Precision.HIGHEST)
    liks, dsums = lax.map(one_facet, (sums.reshape(-1, TS, TS), kern_u.reshape(-1, BINS, TS), kern_v.reshape(-1, BINS, TS), vis_data.reshape(-1, BINS, BINS), facet_count.reshape(-1)))
    dsums = dsums.reshape(FROWS, FCOLS, TS, TS)
    dtiles = jnp.einsum("rqt,rqxy->rtxy", mixing, dsums, precision=lax.Precision.HIGHEST)
    dsky = dtiles.transpose(0, 2, 1, 3).reshape(FROWS * TS, TROW * TS)
    grad_fine = dsky + xi_fine
    dmiddle = back(dsky, coef_fine)
    grad_middle = dmiddle + xi_middle
    grad_coarse = back(dmiddle, coef_middle) + xi_coarse
    prior = 0.5 * (jnp.sum(xi_coarse * xi_coarse) + jnp.sum(xi_middle * xi_middle) + jnp.sum(xi_fine * xi_fine))
    potential = (prior + jnp.sum(liks)) / (FROWS * TS * TROW * TS)
    return grad_coarse, grad_middle, grad_fine, potential
```

```python
import functools

import jax
import jax.numpy as jnp
from jax import lax
from jax.experimental import pallas as pl
from jax.experimental.pallas import tpu as pltpu
from jax.sharding import PartitionSpec as P

inv_noise = 0.125
MESH = pl.DeviceIdType.MESH
ROW, LANE = 8, 128
SIDES = [(dx, dy) for dx in (-1, 0, 1) for dy in (-1, 0, 1) if (dx, dy) != (0, 0)]


def f32dot(a, b, contract):
    return lax.dot_general(a, b, ((contract[:1], contract[1:]), ((), ())), preferred_element_type=jnp.float32)


def split(x):
    high = x.astype(jnp.bfloat16)
    return high, (x - high.astype(jnp.float32)).astype(jnp.bfloat16)


def strip(side, size, edge, near):
    if side == 0:
        return edge, size
    if near:
        return (edge, edge) if side < 0 else (size, edge)
    return (0, edge) if side < 0 else (edge + size, edge)


def region(dx, dy, rows, cols, near):
    return (pl.ds(*strip(dx, rows, ROW, near)), pl.ds(*strip(dy, cols, LANE, near)))


class Halo:
    def __init__(self, src, dst, rows, cols, near, send, recv, at):
        gx, gy, m, n = at
        self.dst, self.at = dst, at
        self.copies = []
        for i, (dx, dy) in enumerate(SIDES):
            self.copies.append(
                pltpu.make_async_remote_copy(
                    src_ref=src.at[region(dx, dy, rows, cols, near)],
                    dst_ref=dst.at[region(-dx, -dy, rows, cols, False)],
                    send_sem=send.at[i],
                    recv_sem=recv.at[i],
                    device_id=(lax.rem(gx + dx + m, m), lax.rem(gy + dy + n, n)),
                    device_id_type=MESH,
                )
            )

    def start(self):
        for c in self.copies:
            c.start()

    def wait(self):
        for c in self.copies:
            c.wait()
        gx, gy, m, n = self.at
        dst = self.dst
        rows, cols = dst.shape
        dst[0:ROW, :] = jnp.where(gx > 0, dst[0:ROW, :], 0.0)
        dst[rows - ROW : rows, :] = jnp.where(gx < m - 1, dst[rows - ROW : rows, :], 0.0)
        dst[:, 0:LANE] = jnp.where(gy > 0, dst[:, 0:LANE], 0.0)
        dst[:, cols - LANE : cols] = jnp.where(gy < n - 1, dst[:, cols - LANE : cols], 0.0)


class Exchange:
    def __init__(self, src, dst, send, recv, at, slab):
        self.src, self.dst, self.send, self.recv, self.at, self.slab = src, dst, send, recv, at, slab

    def copy(self, k):
        gx, gy, m, n = self.at
        peer = lax.rem(gy + k, n)
        return pltpu.make_async_remote_copy(
            src_ref=self.src.at[pl.ds(pl.multiple_of(peer * self.slab, self.slab), self.slab), :],
            dst_ref=self.dst.at[pl.ds(pl.multiple_of(gy * self.slab, self.slab), self.slab), :],
            send_sem=self.send.at[k],
            recv_sem=self.recv.at[k],
            device_id=(gx, peer),
            device_id_type=MESH,
        )

    def start(self):
        gx, gy, m, n = self.at

        @pl.loop(1, n)
        def _(k):
            self.copy(k).start()

        own = pl.ds(pl.multiple_of(gy * self.slab, self.slab), self.slab)
        self.dst[own, :] = self.src[own, :]

    def wait(self):
        @pl.loop(1, self.at[3])
        def _(k):
            self.copy(k).wait()


def spread(ref):
    size = ref.shape[0]
    half = size // 2
    row = lax.broadcasted_iota(jnp.int32, (half, size), 0)
    col = lax.broadcasted_iota(jnp.int32, (half, size), 1)
    ref[0:half, :] = jnp.where(col == 2 * row, 1.0, 0.0).astype(jnp.bfloat16)
    ref[half:size, :] = jnp.where(col == 2 * row + 1, 1.0, 0.0).astype(jnp.bfloat16)


def refine(pad, wins, coef, rolled, high, low, size, rows):
    width = size + 2 * LANE
    for dj in (-1, 0, 1):
        value = pad[...]
        if dj:
            value = pltpu.roll(value, (-dj) % width, 1)
        rolled[...] = value[:, LANE : LANE + size]
        for di in (-1, 0, 1):
            wins[3 * (di + 1) + dj + 1] = rolled[ROW + di : ROW + di + size, :]

    @pl.loop(0, size // rows)
    def _(step):
        at = pl.multiple_of(step * rows, rows)
        here = pl.ds(at, rows)
        totals = [None] * 4
        for near in range(9):
            window = wins[near, here, :]
            for child in range(4):
                term = coef[child, near, here, :].astype(jnp.float32) * window
                totals[child] = term if near == 0 else totals[child] + term
        for child in range(4):
            a, b = child // 2, child % 2
            there = pl.ds(pl.multiple_of(a * size + at, rows), rows)
            high[there, b * size : (b + 1) * size], low[there, b * size : (b + 1) * size] = split(totals[child])


def interleave(high, low, matrix, laced, size):
    for a in (0, 1):
        rows = slice(a * size, (a + 1) * size)
        value = f32dot(high[rows, :], matrix[...], (1, 0)) + f32dot(low[rows, :], matrix[...], (1, 0))
        for c in range(2 * size // LANE):
            laced[c, pl.ds(a, size, stride=2), :] = value[:, c * LANE : (c + 1) * LANE]


def parent_terms(quads, coef, shifted, result, size, rows):
    width = size + 2 * LANE
    tall = size + 4 * ROW
    for d in range(3):
        shifted[d, 0 : 2 * ROW, :] = jnp.zeros((2 * ROW, width), jnp.float32)
        shifted[d, tall - 2 * ROW : tall, :] = jnp.zeros((2 * ROW, width), jnp.float32)

    @pl.loop(0, size // rows)
    def _(step):
        at = pl.multiple_of(step * rows, rows)
        here = pl.ds(at, rows)
        quad = [
            quads[pl.ds(pl.multiple_of(a * size + at, rows), rows), b * size : (b + 1) * size]
            for a in (0, 1)
            for b in (0, 1)
        ]
        blank = jnp.zeros((rows, LANE), jnp.float32)
        for d in range(3):
            total = None
            for j in range(3):
                part = None
                for child in range(4):
                    term = coef[child, 3 * d + j, here, :].astype(jnp.float32) * quad[child]
                    part = term if child == 0 else part + term
                part = jnp.concatenate([blank, part, blank], axis=1)
                if j != 1:
                    part = pltpu.roll(part, (j - 1) % width, 1)
                total = part if j == 0 else total + part
            shifted[d, pl.ds(pl.multiple_of(at + 2 * ROW, ROW), rows), :] = total

    high = tall - 2 * ROW
    result[...] = (
        shifted[1, ROW : ROW + high, :]
        + shifted[2, ROW - 1 : ROW - 1 + high, :]
        + shifted[0, ROW + 1 : ROW + 1 + high, :]
    )


def fold_rim(result, rim, size):
    full_r, full_c = slice(ROW, ROW + size), slice(LANE, LANE + size)
    for rim_r, own_r in ((slice(0, ROW), slice(ROW, 2 * ROW)), (slice(ROW + size, 2 * ROW + size), slice(size, size + ROW))):
        result[own_r, full_c] += rim[rim_r, full_c]
    for rim_c, own_c in (
        (slice(0, LANE), slice(LANE, 2 * LANE)),
        (slice(LANE + size, 2 * LANE + size), slice(size, size + LANE)),
    ):
        result[full_r, own_c] += rim[full_r, rim_c]
        for rim_r, own_r in (
            (slice(0, ROW), slice(ROW, 2 * ROW)),
            (slice(ROW + size, 2 * ROW + size), slice(size, size + ROW)),
        ):
            result[own_r, own_c] += rim[rim_r, rim_c]


def squares(x):
    return jnp.sum(x * x, axis=0, keepdims=True)


def fold_lanes(x):
    total = x[:, 0:LANE]
    for c in range(1, x.shape[1] // LANE):
        total = total + x[:, c * LANE : (c + 1) * LANE]
    return total


def kernel(
    m, n, cells,
    xi_c, xi_m, xi_f, co_m, co_f, k_u, k_v, v_d, meta, counts,
    g_c, g_m, g_f, pot,
    pad_c, pad_m, xm, xf, cm, cf, ku, kv, vd,
    roll_c, roll_m, win_c, win_m, hi_c, lo_c, hi_m, lo_m, lace_c, lace_m, mat_c, mat_m,
    metas, mix_hi, mix_lo, sky, tiles, sums, fsum, dsum, dslab, back_b, dsky,
    quad_c, quad_m, shift_c, shift_m, res_c, res_m, rim_c, rim_m,
    amp_v, parts, part_y, part_x,
    load, sem_cs, sem_cr, sem_ms, sem_mr, sem_fs, sem_fr, sem_bs, sem_br,
    a2a_s, a2a_r, sem_ts, sem_tr, sem_ys, sem_yr, sem_xs, sem_xr,
):
    gx, gy = lax.axis_index("gx"), lax.axis_index("gy")
    at = (gx, gy, m, n)
    nc, nm, nf = xi_c.shape[0], xi_m.shape[0], xi_f.shape[0]
    slab = nf // n
    facets = k_u.shape[1]
    bins = v_d.shape[2]

    loads = [
        pltpu.make_async_copy(src, dst, load.at[i])
        for i, (src, dst) in enumerate(
            (
                (xi_c, pad_c.at[ROW : ROW + nc, LANE : LANE + nc]),
                (co_m, cm),
                (xi_m, xm),
                (co_f, cf),
                (xi_f, xf),
                (k_u.at[0], ku),
                (k_v.at[0], kv),
                (v_d.at[0], vd),
            )
        )
    ]
    for c in loads:
        c.start()

    barrier = pltpu.get_barrier_semaphore()
    greeted = 0
    for k in range(1, n):
        pl.semaphore_signal(barrier, inc=1, device_id=(gx, lax.rem(gy + k, n)), device_id_type=MESH)
        greeted += 1
    for k in range(1, m):
        pl.semaphore_signal(barrier, inc=1, device_id=(lax.rem(gx + k, m), gy), device_id_type=MESH)
        greeted += 1
    for dx in (-1, 1):
        for dy in (-1, 1):
            pl.semaphore_signal(
                barrier, inc=1, device_id=(lax.rem(gx + dx + m, m), lax.rem(gy + dy + n, n)), device_id_type=MESH
            )
            greeted += 1
    loads[0].wait()
    pl.semaphore_wait(barrier, greeted)

    halo_c = Halo(pad_c, pad_c, nc, nc, True, sem_cs, sem_cr, at)
    halo_c.start()

    def meta_copy(k):
        return pltpu.make_async_remote_copy(
            src_ref=meta,
            dst_ref=metas.at[gy],
            send_sem=sem_ts.at[k],
            recv_sem=sem_tr.at[k],
            device_id=(gx, lax.rem(gy + k, n)),
            device_id_type=MESH,
        )

    @pl.loop(1, n)
    def _(k):
        meta_copy(k).start()

    metas[gy] = meta[...]
    spread(mat_c)
    spread(mat_m)

    loads[1].wait()
    loads[2].wait()
    halo_c.wait()
    refine(pad_c, win_c, cm, roll_c, hi_c, lo_c, nc, 32)
    interleave(hi_c, lo_c, mat_c, lace_c, nc)
    for c in range(nm // LANE):
        cols = slice(c * LANE, (c + 1) * LANE)
        pad_m[ROW : ROW + nm, LANE + c * LANE : LANE + (c + 1) * LANE] = lace_c[c] + xm[:, cols]
    halo_m = Halo(pad_m, pad_m, nm, nm, True, sem_ms, sem_mr, at)
    halo_m.start()

    @pl.loop(1, n)
    def _(k):
        meta_copy(k).wait()

    lane = lax.broadcasted_iota(jnp.int32, (slab, nf), 1)
    row = lax.broadcasted_iota(jnp.int32, (slab, nf), 0)
    tile_of = (lane // slab).astype(jnp.float32)
    same = lane % slab == row

    @pl.loop(0, n)
    def _(o):
        rows = pl.ds(pl.multiple_of(o * slab, slab), slab)
        value = metas[o]
        for f in range(facets):
            total = jnp.zeros((slab, nf), jnp.float32)
            for s in range(2):
                i = 2 * f + s
                tile = jnp.concatenate([value[i : i + 1, :]] * (nf // LANE), axis=1)
                weight = jnp.concatenate([value[4 + i : 5 + i, :]] * (nf // LANE), axis=1)
                total = total + jnp.where((tile == tile_of) & same, weight, 0.0)
            mix_hi[f, rows, :], mix_lo[f, rows, :] = split(total)

    loads[3].wait()
    loads[4].wait()
    halo_m.wait()
    refine(pad_m, win_m, cf, roll_m, hi_m, lo_m, nm, 16)
    interleave(hi_m, lo_m, mat_m, lace_m, nm)
    for c in range(nf // LANE):
        cols = slice(c * LANE, (c + 1) * LANE)
        sky[:, cols] = (lace_m[c] + xf[:, cols]).astype(jnp.bfloat16)

    def exchange(i, src, dst):
        return Exchange(src, dst, a2a_s.at[i], a2a_r.at[i], at, slab)

    first = exchange(0, sky, tiles)
    first.start()
    prior = fold_lanes(squares(pad_c[ROW : ROW + nc, LANE : LANE + nc]))
    prior = prior + fold_lanes(squares(xm[...])) + fold_lanes(squares(xf[...]))
    parts[...] = jnp.zeros_like(parts)
    first.wait()
    out = []
    for f in range(facets):
        sums[f] = (f32dot(mix_hi[f], tiles[...], (1, 0)) + f32dot(mix_lo[f], tiles[...], (1, 0))).astype(jnp.bfloat16)
        out.append(exchange(1 + f, sums.at[f], fsum.at[f]))
        out[f].start()

    loads[5].wait()
    loads[6].wait()
    loads[7].wait()
    home = []
    chunk = 256
    for f in range(facets):
        out[f].wait()
        count = counts[0, f]
        amp_v[...] = jnp.zeros_like(amp_v)

        @pl.loop(0, bins // chunk)
        def _(step):
            here = pl.ds(pl.multiple_of(step * chunk, chunk), chunk)
            u = ku[f, here, :]
            amp = f32dot(u, fsum[f], (1, 0)).astype(jnp.bfloat16)
            vis = f32dot(amp, kv[f], (1, 1))
            bin_at = step * chunk + lax.broadcasted_iota(jnp.int32, (chunk, bins), 0)
            resid = jnp.where(bin_at < count, vis - vd[f, here, :].astype(jnp.float32), 0.0)
            parts[...] += squares(resid)
            dvis = (inv_noise * resid).astype(jnp.bfloat16)
            damp = f32dot(dvis, kv[f], (1, 0)).astype(jnp.bfloat16)
            amp_v[...] += f32dot(u, damp, (0, 0))

        dsum[f] = amp_v[...].astype(jnp.bfloat16)
        home.append(exchange(1 + facets + f, dsum.at[f], dslab.at[f]))
        home[f].start()

    own = 0.5 * prior + 0.5 * inv_noise * fold_lanes(parts[...])
    part_y[gy] = jnp.where(lax.broadcasted_iota(jnp.int32, (ROW, LANE), 0) == 0, own, 0.0)

    def pot_y(k):
        return pltpu.make_async_remote_copy(
            src_ref=part_y.at[gy],
            dst_ref=part_y.at[gy],
            send_sem=sem_ys.at[k],
            recv_sem=sem_yr.at[k],
            device_id=(gx, lax.rem(gy + k, n)),
            device_id_type=MESH,
        )

    def pot_x(k):
        return pltpu.make_async_remote_copy(
            src_ref=part_x.at[gx],
            dst_ref=part_x.at[gx],
            send_sem=sem_xs.at[k],
            recv_sem=sem_xr.at[k],
            device_id=(lax.rem(gx + k, m), gy),
            device_id_type=MESH,
        )

    @pl.loop(1, n)
    def _(k):
        pot_y(k).start()

    for f in range(facets):
        home[f].wait()
        part = f32dot(mix_hi[f], dslab[f], (0, 0)) + f32dot(mix_lo[f], dslab[f], (0, 0))
        if f == 0:
            amp_v[...] = part
        else:
            amp_v[...] += part
    back_b[...] = amp_v[...].astype(jnp.bfloat16)
    last = exchange(1 + 2 * facets, back_b, dsky)
    last.start()

    @pl.loop(1, n)
    def _(k):
        pot_y(k).wait()

    part_x[gx] = jnp.sum(part_y[...], axis=0)

    @pl.loop(1, m)
    def _(k):
        pot_x(k).start()

    last.wait()
    for a in (0, 1):
        rows = slice(a * nm, (a + 1) * nm)
        lined = f32dot(mat_m[rows, :], dsky[...], (1, 0)).astype(jnp.bfloat16)
        quad_m[rows, :] = f32dot(lined, mat_m[...], (1, 1))
    parent_terms(quad_m, cf, shift_m, res_m, nm, 16)
    halo_f = Halo(res_m, rim_m, nm, nm, False, sem_fs, sem_fr, at)
    halo_f.start()
    g_f[...] = dsky[...].astype(jnp.float32) + xf[...]
    halo_f.wait()
    fold_rim(res_m, rim_m, nm)
    dmiddle = res_m[ROW : ROW + nm, LANE : LANE + nm]
    g_m[...] = dmiddle + xm[...]
    high, low = split(dmiddle)
    for a in (0, 1):
        rows = slice(a * nc, (a + 1) * nc)
        matrix = mat_c[rows, :]
        quad_c[rows, :] = f32dot(
            f32dot(matrix, high, (1, 0)).astype(jnp.bfloat16), mat_c[...], (1, 1)
        ) + f32dot(f32dot(matrix, low, (1, 0)).astype(jnp.bfloat16), mat_c[...], (1, 1))
    parent_terms(quad_c, cm, shift_c, res_c, nc, 32)
    halo_b = Halo(res_c, rim_c, nc, nc, False, sem_bs, sem_br, at)
    halo_b.start()

    @pl.loop(1, m)
    def _(k):
        pot_x(k).wait()

    pot[0, 0] = jnp.sum(part_x[...]) / cells
    halo_b.wait()
    fold_rim(res_c, rim_c, nc)
    g_c[...] = res_c[ROW : ROW + nc, LANE : LANE + nc] + pad_c[ROW : ROW + nc, LANE : LANE + nc]


def body(
    xi_coarse, xi_middle, xi_fine, coef_middle, coef_fine, kern_u, kern_v, vis_data, facet_tiles, facet_weight, facet_count
):
    m, n = lax.axis_size("gx"), lax.axis_size("gy")
    nc, nm, nf = xi_coarse.shape[0], xi_middle.shape[0], xi_fine.shape[0]
    facets, bins = kern_u.shape[1], vis_data.shape[2]
    cells = float(m * n * nf * nf)
    meta = jnp.concatenate([facet_tiles.reshape(4).astype(jnp.float32), facet_weight.reshape(4)])
    meta = jnp.broadcast_to(meta[:, None], (8, LANE))
    f32, bf16 = jnp.float32, jnp.bfloat16
    vmem, dma = pltpu.VMEM, pltpu.SemaphoreType.DMA

    def wide(size):
        return vmem((size + 2 * ROW, size + 2 * LANE), f32)

    scratch = [
        wide(nc), wide(nm), vmem((nm, nm), f32), vmem((nf, nf), f32),
        vmem(coef_middle.shape, bf16), vmem(coef_fine.shape, bf16),
        vmem(kern_u.shape[1:], bf16), vmem(kern_v.shape[1:], bf16), vmem(vis_data.shape[1:], bf16),
        vmem((nc + 2 * ROW, nc), f32), vmem((nm + 2 * ROW, nm), f32),
        vmem((9, nc, nc), f32), vmem((9, nm, nm), f32),
        vmem((nm, nm), bf16), vmem((nm, nm), bf16), vmem((nf, nf), bf16), vmem((nf, nf), bf16),
        vmem((nm // LANE, nm, LANE), f32), vmem((nf // LANE, nf, LANE), f32),
        vmem((nm, nm), bf16), vmem((nf, nf), bf16),
        vmem((n, 8, LANE), f32), vmem((facets, nf, nf), bf16), vmem((facets, nf, nf), bf16),
        vmem((nf, nf), bf16), vmem((nf, nf), bf16),
        vmem((facets, nf, nf), bf16), vmem((facets, nf, nf), bf16),
        vmem((facets, nf, nf), bf16), vmem((facets, nf, nf), bf16),
        vmem((nf, nf), bf16), vmem((nf, nf), bf16),
        vmem((nm, nm), f32), vmem((nf, nf), f32),
        vmem((3, nc + 4 * ROW, nc + 2 * LANE), f32), vmem((3, nm + 4 * ROW, nm + 2 * LANE), f32),
        wide(nc), wide(nm), wide(nc), wide(nm),
        vmem((nf, nf), f32), vmem((1, bins), f32), vmem((n, 8, LANE), f32), vmem((m, 8, LANE), f32),
        dma((8,)),
        *[dma((8,)) for _ in range(8)],
        dma((2 + 2 * facets, n)), dma((2 + 2 * facets, n)),
        dma((n,)), dma((n,)), dma((n,)), dma((n,)), dma((m,)), dma((m,)),
    ]
    hbm = pl.BlockSpec(memory_space=pl.ANY)
    here = pl.BlockSpec(memory_space=pltpu.VMEM)
    small = pl.BlockSpec(memory_space=pltpu.SMEM)
    grads = pl.pallas_call(
        functools.partial(kernel, m, n, cells),
        name="prior_gradient",
        out_shape=(
            jax.ShapeDtypeStruct(xi_coarse.shape, f32),
            jax.ShapeDtypeStruct(xi_middle.shape, f32),
            jax.ShapeDtypeStruct(xi_fine.shape, f32),
            jax.ShapeDtypeStruct((1, 1), f32),
        ),
        in_specs=[hbm] * 8 + [here, small],
        out_specs=(here, here, here, small),
        scratch_shapes=scratch,
        compiler_params=pltpu.CompilerParams(
            collective_id=0, has_side_effects=True, vmem_limit_bytes=60 * 1024 * 1024
        ),
    )(xi_coarse, xi_middle, xi_fine, coef_middle, coef_fine, kern_u, kern_v, vis_data, meta, facet_count)
    return (*grads[:3], grads[3].reshape(()))


def solution(mesh):
    placed = (
        P("gx", "gy"),
        P("gx", "gy"),
        P("gx", "gy"),
        P(None, None, "gx", "gy"),
        P(None, None, "gx", "gy"),
        P("gx", "gy", None, None),
        P("gx", "gy", None, None),
        P("gx", "gy", None, None),
        P("gx", "gy", None),
        P("gx", "gy", None),
        P("gx", "gy"),
    )
    return jax.shard_map(
        body,
        mesh=mesh,
        in_specs=placed,
        out_specs=(P("gx", "gy"), P("gx", "gy"), P("gx", "gy"), P()),
        check_vma=False,
    )
```

```python
import functools

import jax
import jax.numpy as jnp
from jax import lax
from jax.experimental import pallas as pl
from jax.experimental.pallas import tpu as pltpu
from jax.sharding import PartitionSpec as P

inv_noise = 0.125
MESH = pl.DeviceIdType.MESH
ROW, LANE = 8, 128
SIDES = [(dx, dy) for dx in (-1, 0, 1) for dy in (-1, 0, 1) if (dx, dy) != (0, 0)]


def f32dot(a, b, contract):
    return lax.dot_general(a, b, ((contract[:1], contract[1:]), ((), ())), preferred_element_type=jnp.float32)


def split(x):
    high = x.astype(jnp.bfloat16)
    return high, (x - high.astype(jnp.float32)).astype(jnp.bfloat16)


def strip(side, size, edge, near):
    if side == 0:
        return edge, size
    if near:
        return (edge, edge) if side < 0 else (size, edge)
    return (0, edge) if side < 0 else (edge + size, edge)


def diagonal():
    row = lax.broadcasted_iota(jnp.int32, (LANE, LANE), 0)
    return row == lax.broadcasted_iota(jnp.int32, (LANE, LANE), 1)


class Halo:
    def __init__(self, src, rows_in, cols_out, cols_in, near, send, recv, at):
        gx, gy, m, n = at
        self.src, self.rows_in, self.cols_out, self.cols_in, self.near, self.at = src, rows_in, cols_out, cols_in, near, at
        self.size = size = src.shape[0] - 2 * ROW
        self.copies = []
        for i, (dx, dy) in enumerate(SIDES):
            side = 0 if max(dx, -1) > 0 or (dx == 0 and dy > 0) else 1
            if dx:
                source = src.at[pl.ds(*strip(dx, size, ROW, near)), pl.ds(*strip(dy, size, LANE, near))]
                target = rows_in.at[side, :, pl.ds(*strip(-dy, size, LANE, False))]
            else:
                source, target = cols_out.at[side], cols_in.at[side]
            self.copies.append(
                pltpu.make_async_remote_copy(
                    src_ref=source,
                    dst_ref=target,
                    send_sem=send.at[i],
                    recv_sem=recv.at[i],
                    device_id=(lax.rem(gx + dx + m, m), lax.rem(gy + dy + n, n)),
                    device_id_type=MESH,
                )
            )

    def start(self):
        size, eye = self.size, diagonal()
        for side, dy in ((0, 1), (1, -1)):
            lane = (LANE + size - 1 if dy > 0 else LANE) if self.near else (LANE + size if dy > 0 else LANE - 1)
            tile = lane // LANE * LANE
            for b in range(size // LANE):
                block = self.src[ROW + b * LANE : ROW + (b + 1) * LANE, tile : tile + LANE]
                block = jnp.broadcast_to(block[:, lane - tile : lane - tile + 1], (LANE, LANE))
                self.cols_out[side, b : b + 1, :] = jnp.sum(jnp.where(eye, block, 0.0), axis=0, keepdims=True)
        for c in self.copies:
            c.start()

    def wait(self):
        for c in self.copies:
            c.wait()

    def column(self, side):
        gx, gy, m, n = self.at
        inside = gy > 0 if side == 0 else gy < n - 1
        blocks = []
        for b in range(self.size // LANE):
            block = jnp.broadcast_to(self.cols_in[side, b : b + 1, :], (LANE, LANE))
            blocks.append(jnp.sum(jnp.where(diagonal(), block, 0.0), axis=1, keepdims=True))
        return jnp.where(inside, jnp.concatenate(blocks, axis=0), 0.0)

    def strips(self, side):
        gx, gy, m, n = self.at
        inside = gx > 0 if side == 0 else gx < m - 1
        value = jnp.where(inside, self.rows_in[side], 0.0)
        left, right = value[:, 0:LANE], value[:, LANE + self.size : 2 * LANE + self.size]
        return jnp.where(gy > 0, left, 0.0), value[:, LANE : LANE + self.size], jnp.where(gy < n - 1, right, 0.0)

    def surround(self, pad):
        size = self.size
        for side, start in ((0, 0), (1, ROW + size)):
            pad[start : start + ROW, :] = jnp.concatenate(self.strips(side), axis=1)
        for side, start in ((0, 0), (1, LANE + size)):
            pad[ROW : ROW + size, start : start + LANE] = jnp.broadcast_to(self.column(side), (size, LANE))

    def fold(self, result):
        size = self.size
        first, last = slice(LANE, 2 * LANE), slice(size, size + LANE)
        for side, rows in ((0, slice(ROW, 2 * ROW)), (1, slice(size, size + ROW))):
            left, middle, right = self.strips(side)
            result[rows, LANE : LANE + size] += middle
            result[rows, first] += left
            result[rows, last] += right
        lane = lax.broadcasted_iota(jnp.int32, (size, LANE), 1)
        full = slice(ROW, ROW + size)
        result[full, first] += jnp.where(lane == 0, self.column(0), 0.0)
        result[full, last] += jnp.where(lane == LANE - 1, self.column(1), 0.0)


class Exchange:
    def __init__(self, src, dst, send, recv, at, slab, cols=None):
        self.src, self.dst, self.send, self.recv, self.at, self.slab = src, dst, send, recv, at, slab
        self.cols = slice(0, src.shape[1]) if cols is None else cols

    def rows(self, index):
        return pl.ds(pl.multiple_of(index * self.slab, self.slab), self.slab)

    def copy(self, k):
        gx, gy, m, n = self.at
        peer = lax.rem(gy + k, n)
        return pltpu.make_async_remote_copy(
            src_ref=self.src.at[self.rows(peer), self.cols],
            dst_ref=self.dst.at[self.rows(gy), self.cols],
            send_sem=self.send.at[k],
            recv_sem=self.recv.at[k],
            device_id=(gx, peer),
            device_id_type=MESH,
        )

    def own(self):
        here = self.rows(self.at[1])
        self.dst[here, self.cols] = self.src[here, self.cols]

    def start(self):
        @pl.loop(1, self.at[3])
        def _(k):
            self.copy(k).start()

        self.own()

    def wait(self):
        @pl.loop(1, self.at[3])
        def _(k):
            self.copy(k).wait()

    def meets(self, index, ends):
        n = self.at[3]
        at_end = (index == 0) | (index == n - 1)
        return at_end if ends else jnp.logical_not(at_end)

    def start_some(self, low, high, ends):
        gx, gy, m, n = self.at

        @pl.loop(low, high)
        def _(k):
            @pl.when(self.meets(lax.rem(gy + k, n), ends))
            def _():
                self.copy(k).start()

    def wait_some(self, ends):
        gx, gy, m, n = self.at

        @pl.loop(1, n)
        def _(k):
            @pl.when(self.meets(lax.rem(gy + k, n), ends))
            def _():
                self.copy(k).wait_send()

        @pl.when(self.meets(gy, ends))
        def _():
            @pl.loop(1, n)
            def _(k):
                self.copy(k).wait_recv()


def spread(ref):
    size = ref.shape[0]
    half = size // 2
    row = lax.broadcasted_iota(jnp.int32, (half, size), 0)
    col = lax.broadcasted_iota(jnp.int32, (half, size), 1)
    ref[0:half, :] = jnp.where(col == 2 * row, 1.0, 0.0).astype(jnp.bfloat16)
    ref[half:size, :] = jnp.where(col == 2 * row + 1, 1.0, 0.0).astype(jnp.bfloat16)


def refine(pad, wins, coef, rolled, high, low, size, rows):
    width = size + 2 * LANE
    for dj in (-1, 0, 1):
        value = pad[...]
        if dj:
            value = pltpu.roll(value, (-dj) % width, 1)
        rolled[...] = value[:, LANE : LANE + size]
        for di in (-1, 0, 1):
            wins[3 * (di + 1) + dj + 1] = rolled[ROW + di : ROW + di + size, :]

    @pl.loop(0, size // rows)
    def _(step):
        at = pl.multiple_of(step * rows, rows)
        here = pl.ds(at, rows)
        totals = [None] * 4
        for near in range(9):
            window = wins[near, here, :]
            for child in range(4):
                term = coef[child, near, here, :].astype(jnp.float32) * window
                totals[child] = term if near == 0 else totals[child] + term
        for child in range(4):
            a, b = child // 2, child % 2
            there = pl.ds(pl.multiple_of(a * size + at, rows), rows)
            high[there, b * size : (b + 1) * size], low[there, b * size : (b + 1) * size] = split(totals[child])


def interleave(high, low, matrix, laced, size):
    for a in (0, 1):
        rows = slice(a * size, (a + 1) * size)
        value = f32dot(high[rows, :], matrix[...], (1, 0)) + f32dot(low[rows, :], matrix[...], (1, 0))
        for c in range(2 * size // LANE):
            laced[c, pl.ds(a, size, stride=2), :] = value[:, c * LANE : (c + 1) * LANE]


def parent_terms(quads, coef, shifted, result, size, rows):
    width = size + 2 * LANE
    tall = size + 4 * ROW
    for d in range(3):
        shifted[d, 0 : 2 * ROW, :] = jnp.zeros((2 * ROW, width), jnp.float32)
        shifted[d, tall - 2 * ROW : tall, :] = jnp.zeros((2 * ROW, width), jnp.float32)

    @pl.loop(0, size // rows)
    def _(step):
        at = pl.multiple_of(step * rows, rows)
        here = pl.ds(at, rows)
        quad = [
            quads[pl.ds(pl.multiple_of(a * size + at, rows), rows), b * size : (b + 1) * size]
            for a in (0, 1)
            for b in (0, 1)
        ]
        blank = jnp.zeros((rows, LANE), jnp.float32)
        for d in range(3):
            total = None
            for j in range(3):
                part = None
                for child in range(4):
                    term = coef[child, 3 * d + j, here, :].astype(jnp.float32) * quad[child]
                    part = term if child == 0 else part + term
                part = jnp.concatenate([blank, part, blank], axis=1)
                if j != 1:
                    part = pltpu.roll(part, (j - 1) % width, 1)
                total = part if j == 0 else total + part
            shifted[d, pl.ds(pl.multiple_of(at + 2 * ROW, ROW), rows), :] = total

    high = tall - 2 * ROW
    result[...] = (
        shifted[1, ROW : ROW + high, :]
        + shifted[2, ROW - 1 : ROW - 1 + high, :]
        + shifted[0, ROW + 1 : ROW + 1 + high, :]
    )


def squares(x):
    return jnp.sum(x * x, axis=0, keepdims=True)


def fold_lanes(x):
    total = x[:, 0:LANE]
    for c in range(1, x.shape[1] // LANE):
        total = total + x[:, c * LANE : (c + 1) * LANE]
    return total


def kernel(
    m, n, cells,
    xi_c, xi_m, xi_f, co_m, co_f, k_u, k_v, v_d, listed, weights, counts,
    g_c, g_m, g_f, pot,
    pad_c, pad_m, xm, xf, cm, cf, ku, kv, vd, kut,
    roll_c, roll_m, win_c, win_m, hi_c, lo_c, hi_m, lo_m, lace_c, lace_m, mat_c, mat_m,
    meta, metas, mix_hi, mix_lo, sky, sky_2, edge, edges, tiles, sums, fsum, damps, dsum, dslab, back_b, dsky,
    quad_c, quad_m, shift_c, shift_m, res_c, res_m, grad_c, grad_m, grad_f, back_v,
    row_c, row_m, row_f, row_b, col_o, col_i,
    parts, part_y, part_x,
    load, save, sem_s, sem_r, a2a_s, a2a_r, sem_ts, sem_tr, sem_ys, sem_yr, sem_xs, sem_xr,
):
    gx, gy = lax.axis_index("gx"), lax.axis_index("gy")
    at = (gx, gy, m, n)
    nc, nm, nf = xi_c.shape[0], xi_m.shape[0], xi_f.shape[0]
    slab = nf // n
    facets = k_u.shape[1]
    bins = v_d.shape[2]

    barrier = pltpu.get_barrier_semaphore()
    greeted = 0
    for dx in (-1, 1):
        for dy in (-1, 1):
            pl.semaphore_signal(
                barrier, inc=1, device_id=(lax.rem(gx + dx + m, m), lax.rem(gy + dy + n, n)), device_id_type=MESH
            )
            greeted += 1
    for k in range(1, m):
        pl.semaphore_signal(barrier, inc=1, device_id=(lax.rem(gx + k, m), gy), device_id_type=MESH)
        greeted += 1
    for k in range(1, n):
        pl.semaphore_signal(barrier, inc=1, device_id=(gx, lax.rem(gy + k, n)), device_id_type=MESH)
        greeted += 1

    loads = [
        pltpu.make_async_copy(src, dst, load.at[i])
        for i, (src, dst) in enumerate(
            (
                (xi_c, pad_c.at[ROW : ROW + nc, LANE : LANE + nc]),
                (co_m, cm),
                (xi_m, xm),
                (co_f, cf),
                (xi_f, xf),
                (k_u.at[0], ku),
                (k_v.at[0], kv),
                (v_d.at[0], vd),
            )
        )
    ]
    for c in loads:
        c.start()

    def blank(pad, size):
        width = size + 2 * LANE
        pad[0:ROW, :] = jnp.zeros((ROW, width), jnp.float32)
        pad[ROW + size : 2 * ROW + size, :] = jnp.zeros((ROW, width), jnp.float32)
        pad[ROW : ROW + size, 0:LANE] = jnp.zeros((size, LANE), jnp.float32)
        pad[ROW : ROW + size, LANE + size : width] = jnp.zeros((size, LANE), jnp.float32)

    def middle_level():
        refine(pad_c, win_c, cm, roll_c, hi_c, lo_c, nc, 32)
        interleave(hi_c, lo_c, mat_c, lace_c, nc)
        for c in range(nm // LANE):
            cols = slice(c * LANE, (c + 1) * LANE)
            pad_m[ROW : ROW + nm, LANE + c * LANE : LANE + (c + 1) * LANE] = lace_c[c] + xm[:, cols]

    def fine_level(out):
        refine(pad_m, win_m, cf, roll_m, hi_m, lo_m, nm, 16)
        interleave(hi_m, lo_m, mat_m, lace_m, nm)
        for c in range(nf // LANE):
            cols = slice(c * LANE, (c + 1) * LANE)
            out[:, cols] = (lace_m[c] + xf[:, cols]).astype(jnp.bfloat16)

    def halo(i, src, rows_in, near):
        return Halo(src, rows_in, col_o.at[i], col_i.at[i], near, sem_s.at[i], sem_r.at[i], at)

    def exchange(i, src, dst, cols=None):
        return Exchange(src, dst, a2a_s.at[i], a2a_r.at[i], at, slab, cols)

    spread(mat_c)
    spread(mat_m)
    blank(pad_c, nc)
    blank(pad_m, nm)
    for f in range(facets):
        for s in range(2):
            i = 2 * f + s
            meta[i : i + 1, :] = jnp.full((1, LANE), listed[0, f, s].astype(jnp.float32))
            meta[4 + i : 5 + i, :] = jnp.full((1, LANE), weights[0, f, s])
    for c in loads[:3]:
        c.wait()
    middle_level()
    col_o[...] = jnp.zeros_like(col_o)
    pl.semaphore_wait(barrier, greeted)

    halo_c = halo(0, pad_c, row_c, True)
    halo_c.start()

    def meta_copy(k):
        return pltpu.make_async_remote_copy(
            src_ref=meta,
            dst_ref=metas.at[gy],
            send_sem=sem_ts.at[k],
            recv_sem=sem_tr.at[k],
            device_id=(gx, lax.rem(gy + k, n)),
            device_id_type=MESH,
        )

    @pl.loop(1, n)
    def _(k):
        meta_copy(k).start()

    metas[gy] = meta[...]
    for c in loads[3:5]:
        c.wait()
    fine_level(sky)
    early = exchange(0, sky, tiles)
    early.start_some(1, n // 2, False)

    halo_c.wait()
    halo_c.surround(pad_c)
    middle_level()
    halo_m = halo(1, pad_m, row_m, True)
    halo_m.start()
    early.start_some(n // 2, n, False)

    @pl.loop(1, n)
    def _(k):
        meta_copy(k).wait()

    lane = lax.broadcasted_iota(jnp.int32, (slab, nf), 1)
    row = lax.broadcasted_iota(jnp.int32, (slab, nf), 0)
    tile_of = (lane // slab).astype(jnp.float32)
    same = lane % slab == row

    @pl.loop(0, n)
    def _(o):
        rows = pl.ds(pl.multiple_of(o * slab, slab), slab)
        value = metas[o]
        for f in range(facets):
            total = jnp.zeros((slab, nf), jnp.float32)
            for s in range(2):
                i = 2 * f + s
                tile = jnp.concatenate([value[i : i + 1, :]] * (nf // LANE), axis=1)
                weight = jnp.concatenate([value[4 + i : 5 + i, :]] * (nf // LANE), axis=1)
                total = total + jnp.where((tile == tile_of) & same, weight, 0.0)
            mix_hi[f, rows, :], mix_lo[f, rows, :] = split(total)

    halo_m.wait()
    halo_m.surround(pad_m)
    fine_level(sky_2)
    left, right = slice(0, LANE), slice(nf - LANE, nf)
    outer = lax.broadcasted_iota(jnp.int32, (nf, LANE), 1) < LANE // 2
    edge[...] = jnp.where(outer, sky_2[:, left], sky_2[:, right])
    late = exchange(1, sky_2, tiles)
    rim = exchange(2, edge, edges)
    late.start_some(1, n, True)
    rim.start()
    late.own()
    prior = fold_lanes(squares(pad_c[ROW : ROW + nc, LANE : LANE + nc]))
    prior = prior + fold_lanes(squares(xm[...])) + fold_lanes(squares(xf[...]))
    parts[...] = jnp.zeros_like(parts)
    early.wait_some(False)
    late.wait_some(True)
    rim.wait()
    tiles[:, left] = jnp.where(outer, edges[...], tiles[:, left])
    tiles[:, right] = jnp.where(outer, tiles[:, right], edges[...])
    out = []
    for f in range(facets):
        sums[f] = (f32dot(mix_hi[f], tiles[...], (1, 0)) + f32dot(mix_lo[f], tiles[...], (1, 0))).astype(jnp.bfloat16)
        out.append(exchange(3 + f, sums.at[f], fsum.at[f]))
        out[f].start()

    for c in loads[5:]:
        c.wait()
    for f in range(facets):
        kut[f] = ku[f].T
    home = []
    chunk = 256
    halves = [slice(h * nf // 2, (h + 1) * nf // 2) for h in (0, 1)]
    for f in range(facets):
        out[f].wait()
        count = counts[0, f]

        @pl.loop(0, bins // chunk)
        def _(step):
            here = pl.ds(pl.multiple_of(step * chunk, chunk), chunk)
            amp = f32dot(ku[f, here, :], fsum[f], (1, 0)).astype(jnp.bfloat16)
            vis = f32dot(amp, kv[f], (1, 1))
            bin_at = step * chunk + lax.broadcasted_iota(jnp.int32, (chunk, bins), 0)
            resid = jnp.where(bin_at < count, vis - vd[f, here, :].astype(jnp.float32), 0.0)
            parts[...] += squares(resid)
            dvis = (inv_noise * resid).astype(jnp.bfloat16)
            damps[here, :] = f32dot(dvis, kv[f], (1, 0)).astype(jnp.bfloat16)

        for h, cols in enumerate(halves):
            dsum[f, :, cols] = f32dot(kut[f], damps[:, cols], (1, 0)).astype(jnp.bfloat16)
            home.append(exchange(3 + facets + 2 * f + h, dsum.at[f], dslab.at[f], cols))
            home[-1].start()

    own = 0.5 * prior + 0.5 * inv_noise * fold_lanes(parts[...])
    part_y[gy] = jnp.where(lax.broadcasted_iota(jnp.int32, (ROW, LANE), 0) == 0, own, 0.0)

    def pot_y(k):
        return pltpu.make_async_remote_copy(
            src_ref=part_y.at[gy],
            dst_ref=part_y.at[gy],
            send_sem=sem_ys.at[k],
            recv_sem=sem_yr.at[k],
            device_id=(gx, lax.rem(gy + k, n)),
            device_id_type=MESH,
        )

    def pot_x(k):
        return pltpu.make_async_remote_copy(
            src_ref=part_x.at[gx],
            dst_ref=part_x.at[gx],
            send_sem=sem_xs.at[k],
            recv_sem=sem_xr.at[k],
            device_id=(lax.rem(gx + k, m), gy),
            device_id_type=MESH,
        )

    @pl.loop(1, n)
    def _(k):
        pot_y(k).start()

    def unmix(f, cols):
        return f32dot(mix_hi[f], dslab[f, :, cols], (0, 0)) + f32dot(mix_lo[f], dslab[f, :, cols], (0, 0))

    for f in range(facets - 1):
        for h, cols in enumerate(halves):
            home[2 * f + h].wait()
            part = unmix(f, cols)
            back_v[:, cols] = part if f == 0 else back_v[:, cols] + part
    last = []
    f = facets - 1
    for h, cols in enumerate(halves):
        home[2 * f + h].wait()
        part = unmix(f, cols)
        back_b[:, cols] = (back_v[:, cols] + part if f else part).astype(jnp.bfloat16)
        last.append(exchange(3 + 3 * facets + h, back_b, dsky, cols))
        last[h].start()

    @pl.loop(1, n)
    def _(k):
        pot_y(k).wait()

    part_x[gx] = jnp.sum(part_y[...], axis=0)

    @pl.loop(1, m)
    def _(k):
        pot_x(k).start()

    for c in last:
        c.wait()
    for a in (0, 1):
        rows = slice(a * nm, (a + 1) * nm)
        lined = f32dot(mat_m[rows, :], dsky[...], (1, 0)).astype(jnp.bfloat16)
        quad_m[rows, :] = f32dot(lined, mat_m[...], (1, 1))
    parent_terms(quad_m, cf, shift_m, res_m, nm, 16)
    halo_f = halo(2, res_m, row_f, False)
    halo_f.start()
    grad_f[...] = dsky[...].astype(jnp.float32) + xf[...]
    save_f = pltpu.make_async_copy(grad_f, g_f, save.at[0])
    save_f.start()
    halo_f.wait()
    halo_f.fold(res_m)
    dmiddle = res_m[ROW : ROW + nm, LANE : LANE + nm]
    high, low = split(dmiddle)
    for a in (0, 1):
        rows = slice(a * nc, (a + 1) * nc)
        matrix = mat_c[rows, :]
        quad_c[rows, :] = f32dot(
            f32dot(matrix, high, (1, 0)).astype(jnp.bfloat16), mat_c[...], (1, 1)
        ) + f32dot(f32dot(matrix, low, (1, 0)).astype(jnp.bfloat16), mat_c[...], (1, 1))
    parent_terms(quad_c, cm, shift_c, res_c, nc, 32)
    halo_b = halo(3, res_c, row_b, False)
    halo_b.start()
    grad_m[...] = res_m[ROW : ROW + nm, LANE : LANE + nm] + xm[...]
    save_m = pltpu.make_async_copy(grad_m, g_m, save.at[1])
    save_m.start()

    @pl.loop(1, m)
    def _(k):
        pot_x(k).wait()

    pot[0, 0] = jnp.sum(part_x[...]) / cells
    halo_b.wait()
    halo_b.fold(res_c)
    grad_c[...] = res_c[ROW : ROW + nc, LANE : LANE + nc] + pad_c[ROW : ROW + nc, LANE : LANE + nc]
    save_c = pltpu.make_async_copy(grad_c, g_c, save.at[2])
    save_c.start()
    save_f.wait()
    save_m.wait()
    save_c.wait()


def finish(*refs):
    count = (len(refs) - 2) // 3
    given, given_out, held = refs[:count], refs[count : 2 * count], refs[2 * count : 3 * count]
    come, go = refs[3 * count :]
    blocks = []
    for a, b, v in zip(given, given_out, held):
        rows = min(LANE, a.shape[0])
        for start in range(0, a.shape[0], rows):
            here = slice(start, start + rows)
            i = len(blocks)
            blocks.append(
                (
                    pltpu.make_async_copy(a.at[here, :], v.at[here, :], come.at[i]),
                    pltpu.make_async_copy(v.at[here, :], b.at[here, :], go.at[i]),
                )
            )
    for read, _ in blocks:
        read.start()
    for read, write in blocks:
        read.wait()
        write.start()
    for _, write in blocks:
        write.wait()


def body(
    xi_coarse, xi_middle, xi_fine, coef_middle, coef_fine, kern_u, kern_v, vis_data, facet_tiles, facet_weight, facet_count
):
    m, n = lax.axis_size("gx"), lax.axis_size("gy")
    nc, nm, nf = xi_coarse.shape[0], xi_middle.shape[0], xi_fine.shape[0]
    facets, bins = kern_u.shape[1], vis_data.shape[2]
    cells = float(m * n * nf * nf)
    f32, bf16 = jnp.float32, jnp.bfloat16
    vmem, dma = pltpu.VMEM, pltpu.SemaphoreType.DMA

    def wide(size):
        return vmem((size + 2 * ROW, size + 2 * LANE), f32)

    def strips(size):
        return vmem((2, ROW, size + 2 * LANE), f32)

    swaps = 5 + 3 * facets
    scratch = [
        wide(nc), wide(nm), vmem((nm, nm), f32), vmem((nf, nf), f32),
        vmem(coef_middle.shape, bf16), vmem(coef_fine.shape, bf16),
        vmem(kern_u.shape[1:], bf16), vmem(kern_v.shape[1:], bf16), vmem(vis_data.shape[1:], bf16),
        vmem((facets, nf, bins), bf16),
        vmem((nc + 2 * ROW, nc), f32), vmem((nm + 2 * ROW, nm), f32),
        vmem((9, nc, nc), f32), vmem((9, nm, nm), f32),
        vmem((nm, nm), bf16), vmem((nm, nm), bf16), vmem((nf, nf), bf16), vmem((nf, nf), bf16),
        vmem((nm // LANE, nm, LANE), f32), vmem((nf // LANE, nf, LANE), f32),
        vmem((nm, nm), bf16), vmem((nf, nf), bf16),
        vmem((8, LANE), f32), vmem((n, 8, LANE), f32), vmem((facets, nf, nf), bf16), vmem((facets, nf, nf), bf16),
        vmem((nf, nf), bf16), vmem((nf, nf), bf16), vmem((nf, LANE), bf16), vmem((nf, LANE), bf16),
        vmem((nf, nf), bf16), vmem((facets, nf, nf), bf16), vmem((facets, nf, nf), bf16),
        vmem((bins, nf), bf16), vmem((facets, nf, nf), bf16), vmem((facets, nf, nf), bf16),
        vmem((nf, nf), bf16), vmem((nf, nf), bf16),
        vmem((nm, nm), f32), vmem((nf, nf), f32),
        vmem((3, nc + 4 * ROW, nc + 2 * LANE), f32), vmem((3, nm + 4 * ROW, nm + 2 * LANE), f32),
        wide(nc), wide(nm), vmem((nc, nc), f32), vmem((nm, nm), f32), vmem((nf, nf), f32), vmem((nf, nf), f32),
        strips(nc), strips(nm), strips(nm), strips(nc), vmem((4, 2, ROW, LANE), f32), vmem((4, 2, ROW, LANE), f32),
        vmem((1, bins), f32), vmem((n, 8, LANE), f32), vmem((m, 8, LANE), f32),
        dma((8,)), dma((3,)), dma((4, 8)), dma((4, 8)),
        dma((swaps, n)), dma((swaps, n)),
        dma((n,)), dma((n,)), dma((n,)), dma((n,)), dma((m,)), dma((m,)),
    ]
    hbm = pl.BlockSpec(memory_space=pl.ANY)
    small = pl.BlockSpec(memory_space=pltpu.SMEM)
    shapes = [jax.ShapeDtypeStruct(x.shape, f32) for x in (xi_coarse, xi_middle, xi_fine)]
    *grads, total = pl.pallas_call(
        functools.partial(kernel, m, n, cells),
        name="prior_gradient",
        out_shape=(*shapes, jax.ShapeDtypeStruct((1, 1), f32)),
        in_specs=[hbm] * 8 + [small] * 3,
        out_specs=(hbm, hbm, hbm, small),
        scratch_shapes=scratch,
        compiler_params=pltpu.CompilerParams(
            collective_id=0, has_side_effects=True, vmem_limit_bytes=62 * 1024 * 1024
        ),
    )(
        xi_coarse, xi_middle, xi_fine, coef_middle, coef_fine, kern_u, kern_v, vis_data,
        facet_tiles, facet_weight, facet_count,
    )
    grads = pl.pallas_call(
        finish,
        name="hand_out",
        out_shape=shapes,
        in_specs=[hbm] * 3,
        out_specs=[hbm] * 3,
        scratch_shapes=[*[vmem(s.shape, f32) for s in shapes], dma((8,)), dma((8,))],
    )(*grads)
    return (*grads, total.reshape(()))


def solution(mesh):
    placed = (
        P("gx", "gy"),
        P("gx", "gy"),
        P("gx", "gy"),
        P(None, None, "gx", "gy"),
        P(None, None, "gx", "gy"),
        P("gx", "gy", None, None),
        P("gx", "gy", None, None),
        P("gx", "gy", None, None),
        P("gx", "gy", None),
        P("gx", "gy", None),
        P("gx", "gy"),
    )
    return jax.shard_map(
        body,
        mesh=mesh,
        in_specs=placed,
        out_specs=(P("gx", "gy"), P("gx", "gy"), P("gx", "gy"), P()),
        check_vma=False,
    )
```

```python
import functools

import jax
import jax.numpy as jnp
from jax import lax
from jax.experimental import pallas as pl
from jax.experimental.pallas import tpu as pltpu
from jax.sharding import PartitionSpec as P

inv_noise = 0.125
MESH = pl.DeviceIdType.MESH
ROW, LANE = 8, 128
END = 16
SIDES = [(dx, dy) for dx in (-1, 0, 1) for dy in (-1, 0, 1) if (dx, dy) != (0, 0)]


def f32dot(a, b, contract):
    return lax.dot_general(a, b, ((contract[:1], contract[1:]), ((), ())), preferred_element_type=jnp.float32)


def split(x):
    high = x.astype(jnp.bfloat16)
    return high, (x - high.astype(jnp.float32)).astype(jnp.bfloat16)


def strip(side, size, edge, near):
    if side == 0:
        return edge, size
    if near:
        return (edge, edge) if side < 0 else (size, edge)
    return (0, edge) if side < 0 else (edge + size, edge)


def diagonal():
    row = lax.broadcasted_iota(jnp.int32, (LANE, LANE), 0)
    return row == lax.broadcasted_iota(jnp.int32, (LANE, LANE), 1)


class Halo:
    def __init__(self, src, rows_in, cols_out, cols_in, near, send, recv, at):
        gx, gy, m, n = at
        self.src, self.rows_in, self.cols_out, self.cols_in, self.near, self.at = src, rows_in, cols_out, cols_in, near, at
        self.size = size = src.shape[0] - 2 * ROW
        self.copies = []
        for i, (dx, dy) in enumerate(SIDES):
            side = 0 if max(dx, -1) > 0 or (dx == 0 and dy > 0) else 1
            if dx:
                source = src.at[pl.ds(*strip(dx, size, ROW, near)), pl.ds(*strip(dy, size, LANE, near))]
                target = rows_in.at[side, :, pl.ds(*strip(-dy, size, LANE, False))]
            else:
                source, target = cols_out.at[side], cols_in.at[side]
            self.copies.append(
                pltpu.make_async_remote_copy(
                    src_ref=source,
                    dst_ref=target,
                    send_sem=send.at[i],
                    recv_sem=recv.at[i],
                    device_id=(lax.rem(gx + dx + m, m), lax.rem(gy + dy + n, n)),
                    device_id_type=MESH,
                )
            )

    def start(self):
        self.pack()
        self.send()

    def pack(self):
        size, eye = self.size, diagonal()
        for side, dy in ((0, 1), (1, -1)):
            lane = (LANE + size - 1 if dy > 0 else LANE) if self.near else (LANE + size if dy > 0 else LANE - 1)
            tile = lane // LANE * LANE
            for b in range(size // LANE):
                block = self.src[ROW + b * LANE : ROW + (b + 1) * LANE, tile : tile + LANE]
                block = jnp.broadcast_to(block[:, lane - tile : lane - tile + 1], (LANE, LANE))
                self.cols_out[side, b : b + 1, :] = jnp.sum(jnp.where(eye, block, 0.0), axis=0, keepdims=True)

    def send(self):
        for c in self.copies:
            c.start()

    def wait(self):
        for c in self.copies:
            c.wait()

    def column(self, side):
        gx, gy, m, n = self.at
        inside = gy > 0 if side == 0 else gy < n - 1
        blocks = []
        for b in range(self.size // LANE):
            block = jnp.broadcast_to(self.cols_in[side, b : b + 1, :], (LANE, LANE))
            blocks.append(jnp.sum(jnp.where(diagonal(), block, 0.0), axis=1, keepdims=True))
        return jnp.where(inside, jnp.concatenate(blocks, axis=0), 0.0)

    def strips(self, side):
        gx, gy, m, n = self.at
        inside = gx > 0 if side == 0 else gx < m - 1
        value = jnp.where(inside, self.rows_in[side], 0.0)
        left, right = value[:, 0:LANE], value[:, LANE + self.size : 2 * LANE + self.size]
        return jnp.where(gy > 0, left, 0.0), value[:, LANE : LANE + self.size], jnp.where(gy < n - 1, right, 0.0)

    def surround(self, pad):
        size = self.size
        for side, start in ((0, 0), (1, ROW + size)):
            before, middle, after = self.strips(side)
            before = jnp.broadcast_to(before[:, LANE - 1 : LANE], (ROW, LANE))
            after = jnp.broadcast_to(after[:, 0:1], (ROW, LANE))
            pad[start : start + ROW, :] = jnp.concatenate([before, middle, after], axis=1)
        for side, start in ((0, 0), (1, LANE + size)):
            pad[ROW : ROW + size, start : start + LANE] = jnp.broadcast_to(self.column(side), (size, LANE))

    def fold(self, result):
        size = self.size
        first, last = slice(LANE, 2 * LANE), slice(size, size + LANE)
        for side, rows in ((0, slice(ROW, 2 * ROW)), (1, slice(size, size + ROW))):
            left, middle, right = self.strips(side)
            result[rows, LANE : LANE + size] += middle
            result[rows, first] += left
            result[rows, last] += right
        lane = lax.broadcasted_iota(jnp.int32, (size, LANE), 1)
        full = slice(ROW, ROW + size)
        result[full, first] += jnp.where(lane == 0, self.column(0), 0.0)
        result[full, last] += jnp.where(lane == LANE - 1, self.column(1), 0.0)


class Exchange:
    def __init__(self, src, dst, send, recv, at, slab, cols=None):
        self.src, self.dst, self.send, self.recv, self.at, self.slab = src, dst, send, recv, at, slab
        self.cols = slice(0, src.shape[1]) if cols is None else cols

    def rows(self, index):
        return pl.ds(pl.multiple_of(index * self.slab, self.slab), self.slab)

    def copy(self, k):
        gx, gy, m, n = self.at
        peer = lax.rem(gy + k, n)
        return pltpu.make_async_remote_copy(
            src_ref=self.src.at[self.rows(peer), self.cols],
            dst_ref=self.dst.at[self.rows(gy), self.cols],
            send_sem=self.send.at[k],
            recv_sem=self.recv.at[k],
            device_id=(gx, peer),
            device_id_type=MESH,
        )

    def own(self):
        here = self.rows(self.at[1])
        self.dst[here, self.cols] = self.src[here, self.cols]

    def start(self):
        @pl.loop(1, self.at[3])
        def _(k):
            self.copy(k).start()

        self.own()

    def wait(self):
        @pl.loop(1, self.at[3])
        def _(k):
            self.copy(k).wait()

    def start_ends(self):
        gy, n = self.at[1], self.at[3]
        self.own()
        for ends in (True, False):

            @pl.loop(1, n)
            def _(k):
                peer = lax.rem(gy + k, n)
                at_end = (peer == 0) | (peer == n - 1)

                @pl.when(at_end if ends else jnp.logical_not(at_end))
                def _():
                    self.copy(k).start()


def spread(ref):
    size = ref.shape[0]
    half = size // 2
    row = lax.broadcasted_iota(jnp.int32, (half, size), 0)
    col = lax.broadcasted_iota(jnp.int32, (half, size), 1)
    ref[0:half, :] = jnp.where(col == 2 * row, 1.0, 0.0).astype(jnp.bfloat16)
    ref[half:size, :] = jnp.where(col == 2 * row + 1, 1.0, 0.0).astype(jnp.bfloat16)


def refine(pad, wins, coef, rolled, high, low, size, rows):
    own = pad[:, LANE : LANE + size]
    lane = lax.broadcasted_iota(jnp.int32, own.shape, 1)
    for dj in (-1, 0, 1):
        value = own
        if dj:
            beyond = pad[:, 0:LANE] if dj < 0 else pad[:, LANE + size : 2 * LANE + size]
            beyond = jnp.concatenate([beyond] * (size // LANE), axis=1)
            value = jnp.where(lane == (0 if dj < 0 else size - 1), beyond, pltpu.roll(own, (-dj) % size, 1))
        rolled[...] = value
        for di in (-1, 0, 1):
            wins[3 * (di + 1) + dj + 1] = rolled[ROW + di : ROW + di + size, :]

    @pl.loop(0, size // rows)
    def _(step):
        at = pl.multiple_of(step * rows, rows)
        here = pl.ds(at, rows)
        totals = [None] * 4
        for near in range(9):
            window = wins[near, here, :]
            for child in range(4):
                term = coef[child, near, here, :].astype(jnp.float32) * window
                totals[child] = term if near == 0 else totals[child] + term
        for child in range(4):
            a, b = child // 2, child % 2
            there = pl.ds(pl.multiple_of(a * size + at, rows), rows)
            high[there, b * size : (b + 1) * size], low[there, b * size : (b + 1) * size] = split(totals[child])


def interleave(high, low, matrix, laced, size):
    for a in (0, 1):
        rows = slice(a * size, (a + 1) * size)
        value = f32dot(high[rows, :], matrix[...], (1, 0)) + f32dot(low[rows, :], matrix[...], (1, 0))
        for c in range(2 * size // LANE):
            laced[c, pl.ds(a, size, stride=2), :] = value[:, c * LANE : (c + 1) * LANE]


def parent_terms(quads, coef, shifted, result, size, rows):
    width = size + 2 * LANE
    tall = size + 4 * ROW
    for d in range(3):
        shifted[d, 0 : 2 * ROW, :] = jnp.zeros((2 * ROW, width), jnp.float32)
        shifted[d, tall - 2 * ROW : tall, :] = jnp.zeros((2 * ROW, width), jnp.float32)

    @pl.loop(0, size // rows)
    def _(step):
        at = pl.multiple_of(step * rows, rows)
        here = pl.ds(at, rows)
        quad = [
            quads[pl.ds(pl.multiple_of(a * size + at, rows), rows), b * size : (b + 1) * size]
            for a in (0, 1)
            for b in (0, 1)
        ]
        lane = lax.broadcasted_iota(jnp.int32, (rows, size), 1)
        for d in range(3):
            parts = []
            for j in range(3):
                part = None
                for child in range(4):
                    term = coef[child, 3 * d + j, here, :].astype(jnp.float32) * quad[child]
                    part = term if child == 0 else part + term
                parts.append(part if j == 1 else pltpu.roll(part, (j - 1) % size, 1))
            total = parts[1] + jnp.where(lane < size - 1, parts[0], 0.0) + jnp.where(lane > 0, parts[2], 0.0)
            before = jnp.where(lane == size - 1, parts[0], 0.0)[:, size - LANE : size]
            after = jnp.where(lane == 0, parts[2], 0.0)[:, 0:LANE]
            total = jnp.concatenate([before, total, after], axis=1)
            shifted[d, pl.ds(pl.multiple_of(at + 2 * ROW, ROW), rows), :] = total

    high = tall - 2 * ROW
    result[...] = (
        shifted[1, ROW : ROW + high, :]
        + shifted[2, ROW - 1 : ROW - 1 + high, :]
        + shifted[0, ROW + 1 : ROW + 1 + high, :]
    )


def squares(x):
    return jnp.sum(x * x, axis=0, keepdims=True)


def fold_lanes(x):
    total = x[:, 0:LANE]
    for c in range(1, x.shape[1] // LANE):
        total = total + x[:, c * LANE : (c + 1) * LANE]
    return total


def kernel(
    m, n, cells,
    xi_c, xi_m, xi_f, co_m, co_f, k_u, k_v, v_d, f_t, f_w, f_c,
    g_c, g_m, g_f, pot,
    pad_c, pad_m, xm, xf, cm, cf, ku, kv, vd, kut,
    roll_c, roll_m, win_c, win_m, hi_c, lo_c, hi_m, lo_m, lace_c, lace_m, mat_c, mat_m,
    listed, weights, counts, total_s, meta, metas, mix_hi, mix_lo, sky, sky_2, edge, edges, lates, tiles, tiles_o, sums, fsum, damps, dsum, dslab, back_b, dsky, dtile, ends,
    quad_c, quad_m, shift_c, shift_m, res_c, res_m, res_r, grad_c, grad_m, grad_f, back_v,
    row_c, row_m, row_f, row_b, col_o, col_i,
    parts, part_y, part_x,
    load, few, save, sem_s, sem_r, a2a_s, a2a_r, sem_ls, sem_lr, sem_es, sem_er, sem_ts, sem_tr, sem_ys, sem_yr, sem_xs, sem_xr,
):
    gx, gy = lax.axis_index("gx"), lax.axis_index("gy")
    at = (gx, gy, m, n)
    nc, nm, nf = xi_c.shape[0], xi_m.shape[0], xi_f.shape[0]
    slab = nf // n
    facets = k_u.shape[1]
    bins = v_d.shape[2]

    barrier = pltpu.get_barrier_semaphore()
    greeted = 0
    for dx in (-1, 1):
        for dy in (-1, 1):
            pl.semaphore_signal(
                barrier, inc=1, device_id=(lax.rem(gx + dx + m, m), lax.rem(gy + dy + n, n)), device_id_type=MESH
            )
            greeted += 1
    for k in range(1, m):
        pl.semaphore_signal(barrier, inc=1, device_id=(lax.rem(gx + k, m), gy), device_id_type=MESH)
        greeted += 1
    for k in range(1, n):
        pl.semaphore_signal(barrier, inc=1, device_id=(gx, lax.rem(gy + k, n)), device_id_type=MESH)
        greeted += 1

    left, right, inside = slice(0, LANE), slice(nf - LANE, nf), slice(LANE, nf - LANE)
    halves = (slice(0, 2 * LANE), slice(2 * LANE, nf))
    moved = ((left, slice(0, LANE)), (right, slice(LANE, 2 * LANE)), (inside, halves[1]))
    small = [
        pltpu.make_async_copy(src, dst, few.at[i])
        for i, (src, dst) in enumerate(((f_t, listed), (f_w, weights), (f_c, counts)))
    ]
    loads = [
        pltpu.make_async_copy(src, dst, load.at[i])
        for i, (src, dst) in enumerate(
            (
                (xi_c, pad_c.at[ROW : ROW + nc, LANE : LANE + nc]),
                (co_m, cm),
                (xi_m, xm),
                (co_f, cf),
                (xi_f, xf),
                (k_u.at[0], ku),
                *((k_v.at[0, :, :, natural], kv.at[:, :, put]) for natural, put in moved),
                (v_d.at[0], vd),
            )
        )
    ]
    for c in loads[:3] + small + loads[3:]:
        c.start()

    def blank(pad, size):
        width = size + 2 * LANE
        pad[0:ROW, :] = jnp.zeros((ROW, width), jnp.float32)
        pad[ROW + size : 2 * ROW + size, :] = jnp.zeros((ROW, width), jnp.float32)
        pad[ROW : ROW + size, 0:LANE] = jnp.zeros((size, LANE), jnp.float32)
        pad[ROW : ROW + size, LANE + size : width] = jnp.zeros((size, LANE), jnp.float32)

    def middle_level():
        refine(pad_c, win_c, cm, roll_c, hi_c, lo_c, nc, 32)
        interleave(hi_c, lo_c, mat_c, lace_c, nc)
        for c in range(nm // LANE):
            cols = slice(c * LANE, (c + 1) * LANE)
            pad_m[ROW : ROW + nm, LANE + c * LANE : LANE + (c + 1) * LANE] = lace_c[c] + xm[:, cols]

    def fine_level(out):
        refine(pad_m, win_m, cf, roll_m, hi_m, lo_m, nm, 16)
        interleave(hi_m, lo_m, mat_m, lace_m, nm)
        for c in range(nf // LANE):
            cols = slice(c * LANE, (c + 1) * LANE)
            out[:, cols] = (lace_m[c] + xf[:, cols]).astype(jnp.bfloat16)

    def halo(i, src, rows_in, near):
        return Halo(src, rows_in, col_o.at[i], col_i.at[i], near, sem_s.at[i], sem_r.at[i], at)

    def exchange(i, src, dst, cols=None):
        return Exchange(src, dst, a2a_s.at[i], a2a_r.at[i], at, slab, cols)

    spread(mat_c)
    spread(mat_m)
    blank(pad_c, nc)
    blank(pad_m, nm)
    for c in small:
        c.wait()
    for f in range(facets):
        for s in range(2):
            i = 2 * f + s
            meta[i : i + 1, :] = jnp.full((1, LANE), listed[0, f, s].astype(jnp.float32))
            meta[4 + i : 5 + i, :] = jnp.full((1, LANE), weights[0, f, s])
    col_o[...] = jnp.zeros_like(col_o)
    loads[0].wait()
    halo_c = halo(0, pad_c, row_c, True)
    halo_c.pack()
    pl.semaphore_wait(barrier, greeted)
    halo_c.send()

    def meta_copy(k):
        return pltpu.make_async_remote_copy(
            src_ref=meta,
            dst_ref=metas.at[gy],
            send_sem=sem_ts.at[k],
            recv_sem=sem_tr.at[k],
            device_id=(gx, lax.rem(gy + k, n)),
            device_id_type=MESH,
        )

    @pl.loop(1, n)
    def _(k):
        meta_copy(k).start()

    metas[gy] = meta[...]
    for c in loads[1:3]:
        c.wait()
    middle_level()
    for c in loads[3:5]:
        c.wait()
    fine_level(sky)
    early = exchange(0, sky, tiles)

    halo_c.wait()
    halo_c.surround(pad_c)
    middle_level()
    halo_m = halo(1, pad_m, row_m, True)
    halo_m.start()
    early.start()

    @pl.loop(1, n)
    def _(k):
        meta_copy(k).wait()

    lane = lax.broadcasted_iota(jnp.int32, (slab, nf), 1)
    row = lax.broadcasted_iota(jnp.int32, (slab, nf), 0)
    tile_of = (lane // slab).astype(jnp.float32)
    same = lane % slab == row

    @pl.loop(0, n)
    def _(o):
        rows = pl.ds(pl.multiple_of(o * slab, slab), slab)
        value = metas[o]
        for f in range(facets):
            total = jnp.zeros((slab, nf), jnp.float32)
            for s in range(2):
                i = 2 * f + s
                tile = jnp.concatenate([value[i : i + 1, :]] * (nf // LANE), axis=1)
                weight = jnp.concatenate([value[4 + i : 5 + i, :]] * (nf // LANE), axis=1)
                total = total + jnp.where((tile == tile_of) & same, weight, 0.0)
            mix_hi[f, rows, :], mix_lo[f, rows, :] = split(total)

    owners = ((0, 0), (1, n - 1))

    def late_copy(e, owner, source):
        return pltpu.make_async_remote_copy(
            src_ref=sky_2.at[pl.ds(owner * slab + e * (slab - END), END), :],
            dst_ref=lates.at[source],
            send_sem=sem_ls.at[e],
            recv_sem=sem_lr.at[source],
            device_id=(gx, owner),
            device_id_type=MESH,
        )

    halo_m.wait()
    halo_m.surround(pad_m)
    fine_level(sky_2)
    outer = lax.broadcasted_iota(jnp.int32, (nf, LANE), 1) < LANE // 2
    edge[...] = jnp.where(outer, sky_2[:, left], sky_2[:, right])
    rim = exchange(1, edge, edges)
    for e, owner in owners:

        @pl.when(gy != owner)
        def _(e=e, owner=owner):
            late_copy(e, owner, gy).start()

        @pl.when(gy == owner)
        def _(e=e, owner=owner):
            lates[owner] = sky_2[owner * slab + e * (slab - END) : owner * slab + e * (slab - END) + END, :]

    rim.start()

    prior = fold_lanes(squares(pad_c[ROW : ROW + nc, LANE : LANE + nc]))
    prior = prior + fold_lanes(squares(xm[...])) + fold_lanes(squares(xf[...]))
    parts[...] = jnp.zeros_like(parts)
    early.wait()
    for e, owner in owners:

        @pl.when(gy != owner)
        def _(e=e, owner=owner):
            late_copy(e, owner, gy).wait_send()

        @pl.when(gy == owner)
        def _(e=e, owner=owner):
            @pl.loop(1, n)
            def _(k):
                late_copy(e, owner, lax.rem(owner + k, n)).wait_recv()

            for i in range(n):
                at_row = i * slab + e * (slab - END)
                tiles[at_row : at_row + END, :] = lates[i]

    rim.wait()
    mixed = jnp.concatenate(
        [jnp.where(outer, edges[...], tiles[:, left]), jnp.where(outer, tiles[:, right], edges[...]), tiles[:, inside]],
        axis=1,
    )
    tiles_o[...] = mixed
    out = []
    for f in range(facets):
        sums[f] = (f32dot(mix_hi[f], tiles_o[...], (1, 0)) + f32dot(mix_lo[f], tiles_o[...], (1, 0))).astype(jnp.bfloat16)
        out.append(exchange(2 + f, sums.at[f], fsum.at[f]))
        out[f].start()

    for c in loads[5:]:
        c.wait()
    for f in range(facets):
        kut[f] = ku[f].T
    home = []
    chunk = 512
    for f in range(facets):
        out[f].wait()
        count = counts[0, f]

        for step in range(bins // chunk):
            here = slice(step * chunk, (step + 1) * chunk)
            amp = f32dot(ku[f, here, :], fsum[f], (1, 0)).astype(jnp.bfloat16)
            vis = f32dot(amp, kv[f], (1, 1))
            bin_at = step * chunk + lax.broadcasted_iota(jnp.int32, (chunk, bins), 0)
            resid = jnp.where(bin_at < count, vis - vd[f, here, :].astype(jnp.float32), 0.0)
            parts[...] += squares(resid)
            dvis = (inv_noise * resid).astype(jnp.bfloat16)
            damps[here, :] = f32dot(dvis, kv[f], (1, 0)).astype(jnp.bfloat16)

        for h, cols in enumerate(halves):
            dsum[f, :, cols] = f32dot(kut[f], damps[:, cols], (1, 0)).astype(jnp.bfloat16)
            going = exchange(2 + facets + 2 * f + h, dsum.at[f], dslab.at[f], cols)
            home.append(going)
            if f < facets - 1 or h == 0:
                going.start()
            else:
                going.start_ends()

    own = 0.5 * prior + 0.5 * inv_noise * fold_lanes(parts[...])
    part_y[gy] = jnp.where(lax.broadcasted_iota(jnp.int32, (ROW, LANE), 0) == 0, own, 0.0)

    def pot_y(k):
        return pltpu.make_async_remote_copy(
            src_ref=part_y.at[gy],
            dst_ref=part_y.at[gy],
            send_sem=sem_ys.at[k],
            recv_sem=sem_yr.at[k],
            device_id=(gx, lax.rem(gy + k, n)),
            device_id_type=MESH,
        )

    def pot_x(k):
        return pltpu.make_async_remote_copy(
            src_ref=part_x.at[gx],
            dst_ref=part_x.at[gx],
            send_sem=sem_xs.at[k],
            recv_sem=sem_xr.at[k],
            device_id=(lax.rem(gx + k, m), gy),
            device_id_type=MESH,
        )

    @pl.loop(1, n)
    def _(k):
        pot_y(k).start()

    def unmix(f, cols):
        return f32dot(mix_hi[f], dslab[f, :, cols], (0, 0)) + f32dot(mix_lo[f], dslab[f, :, cols], (0, 0))

    for f in range(facets - 1):
        for h, cols in enumerate(halves):
            home[2 * f + h].wait()
            part = unmix(f, cols)
            back_v[:, cols] = part if f == 0 else back_v[:, cols] + part
    def ends_copy(e, k):
        peer = lax.rem(gy + k, n)
        return pltpu.make_async_remote_copy(
            src_ref=back_b.at[ends_rows(e, peer), halves[1]],
            dst_ref=ends.at[e],
            send_sem=sem_es.at[e, k],
            recv_sem=sem_er.at[e, k],
            device_id=(gx, peer),
            device_id_type=MESH,
        )

    def ends_rows(e, index):
        return pl.ds(pl.multiple_of(index * slab + e * (slab - END), END), END)

    def ends_start():
        for e, owner in owners:

            @pl.when(gy == owner)
            def _(e=e):
                @pl.loop(1, n)
                def _(k):
                    ends_copy(e, k).start()

                ends[e] = back_b[ends_rows(e, gy), halves[1]]

    def ends_wait():
        for e, owner in owners:

            @pl.when(gy == owner)
            def _(e=e):
                @pl.loop(1, n)
                def _(k):
                    ends_copy(e, k).wait_send()

            @pl.when(gy != owner)
            def _(e=e, owner=owner):
                ends_copy(e, lax.rem(gy - owner + n, n)).wait_recv()

    last = []
    f = facets - 1
    for h, cols in enumerate(halves):
        home[2 * f + h].wait()
        part = unmix(f, cols)
        back_b[:, cols] = (back_v[:, cols] + part if f else part).astype(jnp.bfloat16)
        if h:
            ends_start()
        last.append(exchange(2 + 3 * facets + h, back_b, dsky, cols))
        last[h].start()

    @pl.loop(1, n)
    def _(k):
        pot_y(k).wait()

    part_x[gx] = jnp.sum(part_y[...], axis=0)

    @pl.loop(1, m)
    def _(k):
        pot_x(k).start()

    def adjoint_fine(result):
        for a in (0, 1):
            rows = slice(a * nm, (a + 1) * nm)
            lined = f32dot(mat_m[rows, :], dtile[...], (1, 0)).astype(jnp.bfloat16)
            quad_m[rows, :] = f32dot(lined, mat_m[...], (1, 1))
        parent_terms(quad_m, cf, shift_m, result, nm, 16)

    last[0].wait()
    dtile[:, left] = dsky[:, 0:LANE]
    dtile[:, right] = dsky[:, LANE : 2 * LANE]
    dtile[END : nf - END, inside] = jnp.zeros((nf - 2 * END, nf - 2 * LANE), jnp.bfloat16)
    ends_wait()
    dtile[0:END, inside] = ends[0]
    dtile[nf - END : nf, inside] = ends[1]
    adjoint_fine(res_r)
    halo_f = halo(2, res_r, row_f, False)
    halo_f.start()
    last[1].wait()
    dtile[:, inside] = dsky[:, halves[1]]
    adjoint_fine(res_m)
    grad_f[...] = dtile[...].astype(jnp.float32) + xf[...]
    save_f = pltpu.make_async_copy(grad_f, g_f, save.at[0])
    save_f.start()
    halo_f.wait()
    halo_f.fold(res_m)
    dmiddle = res_m[ROW : ROW + nm, LANE : LANE + nm]
    high, low = split(dmiddle)
    for a in (0, 1):
        rows = slice(a * nc, (a + 1) * nc)
        matrix = mat_c[rows, :]
        quad_c[rows, :] = f32dot(
            f32dot(matrix, high, (1, 0)).astype(jnp.bfloat16), mat_c[...], (1, 1)
        ) + f32dot(f32dot(matrix, low, (1, 0)).astype(jnp.bfloat16), mat_c[...], (1, 1))
    parent_terms(quad_c, cm, shift_c, res_c, nc, 32)
    halo_b = halo(3, res_c, row_b, False)
    halo_b.start()
    grad_m[...] = res_m[ROW : ROW + nm, LANE : LANE + nm] + xm[...]
    save_m = pltpu.make_async_copy(grad_m, g_m, save.at[1])
    save_m.start()

    @pl.loop(1, m)
    def _(k):
        pot_x(k).wait()

    total_s[0, 0] = jnp.sum(part_x[...]) / cells
    save_p = pltpu.make_async_copy(total_s, pot, save.at[3])
    save_p.start()
    halo_b.wait()
    halo_b.fold(res_c)
    grad_c[...] = res_c[ROW : ROW + nc, LANE : LANE + nc] + pad_c[ROW : ROW + nc, LANE : LANE + nc]
    save_c = pltpu.make_async_copy(grad_c, g_c, save.at[2])
    save_c.start()
    save_f.wait()
    save_m.wait()
    save_c.wait()
    save_p.wait()


def finish(*refs):
    count = (len(refs) - 2) // 3
    given, given_out, held = refs[:count], refs[count : 2 * count], refs[2 * count : 3 * count]
    come, go = refs[3 * count :]
    blocks = []
    for a, b, v in zip(given, given_out, held):
        rows = min(LANE, a.shape[0])
        for start in range(0, a.shape[0], rows):
            here = slice(start, start + rows)
            i = len(blocks)
            blocks.append(
                (
                    pltpu.make_async_copy(a.at[here, :], v.at[here, :], come.at[i]),
                    pltpu.make_async_copy(v.at[here, :], b.at[here, :], go.at[i]),
                )
            )
    for read, _ in blocks:
        read.start()
    for read, write in blocks:
        read.wait()
        write.start()
    for _, write in blocks:
        write.wait()


def body(
    xi_coarse, xi_middle, xi_fine, coef_middle, coef_fine, kern_u, kern_v, vis_data, facet_tiles, facet_weight, facet_count
):
    m, n = lax.axis_size("gx"), lax.axis_size("gy")
    nc, nm, nf = xi_coarse.shape[0], xi_middle.shape[0], xi_fine.shape[0]
    facets, bins = kern_u.shape[1], vis_data.shape[2]
    cells = float(m * n * nf * nf)
    f32, bf16 = jnp.float32, jnp.bfloat16
    vmem, dma = pltpu.VMEM, pltpu.SemaphoreType.DMA

    def wide(size):
        return vmem((size + 2 * ROW, size + 2 * LANE), f32)

    def strips(size):
        return vmem((2, ROW, size + 2 * LANE), f32)

    swaps = 4 + 3 * facets
    scratch = [
        wide(nc), wide(nm), vmem((nm, nm), f32), vmem((nf, nf), f32),
        vmem(coef_middle.shape, bf16), vmem(coef_fine.shape, bf16),
        vmem(kern_u.shape[1:], bf16), vmem(kern_v.shape[1:], bf16), vmem(vis_data.shape[1:], bf16),
        vmem((facets, nf, bins), bf16),
        vmem((nc + 2 * ROW, nc), f32), vmem((nm + 2 * ROW, nm), f32),
        vmem((9, nc, nc), f32), vmem((9, nm, nm), f32),
        vmem((nm, nm), bf16), vmem((nm, nm), bf16), vmem((nf, nf), bf16), vmem((nf, nf), bf16),
        vmem((nm // LANE, nm, LANE), f32), vmem((nf // LANE, nf, LANE), f32),
        vmem((nm, nm), bf16), vmem((nf, nf), bf16),
        pltpu.SMEM(facet_tiles.shape, jnp.int32), pltpu.SMEM(facet_weight.shape, f32),
        pltpu.SMEM(facet_count.shape, jnp.int32), pltpu.SMEM((1, 1), f32),
        vmem((8, LANE), f32), vmem((n, 8, LANE), f32), vmem((facets, nf, nf), bf16), vmem((facets, nf, nf), bf16),
        vmem((nf, nf), bf16), vmem((nf, nf), bf16), vmem((nf, LANE), bf16), vmem((nf, LANE), bf16),
        vmem((n, END, nf), bf16), vmem((nf, nf), bf16), vmem((nf, nf), bf16),
        vmem((facets, nf, nf), bf16), vmem((facets, nf, nf), bf16),
        vmem((bins, nf), bf16), vmem((facets, nf, nf), bf16), vmem((facets, nf, nf), bf16),
        vmem((nf, nf), bf16), vmem((nf, nf), bf16), vmem((nf, nf), bf16), vmem((2, END, nf - 2 * LANE), bf16),
        vmem((nm, nm), f32), vmem((nf, nf), f32),
        vmem((3, nc + 4 * ROW, nc + 2 * LANE), f32), vmem((3, nm + 4 * ROW, nm + 2 * LANE), f32),
        wide(nc), wide(nm), wide(nm), vmem((nc, nc), f32), vmem((nm, nm), f32), vmem((nf, nf), f32), vmem((nf, nf), f32),
        strips(nc), strips(nm), strips(nm), strips(nc), vmem((4, 2, ROW, LANE), f32), vmem((4, 2, ROW, LANE), f32),
        vmem((1, bins), f32), vmem((n, 8, LANE), f32), vmem((m, 8, LANE), f32),
        dma((10,)), dma((3,)), dma((4,)), dma((4, 8)), dma((4, 8)),
        dma((swaps, n)), dma((swaps, n)), dma((2,)), dma((n,)), dma((2, n)), dma((2, n)),
        dma((n,)), dma((n,)), dma((n,)), dma((n,)), dma((m,)), dma((m,)),
    ]
    hbm = pl.BlockSpec(memory_space=pl.ANY)
    shapes = [jax.ShapeDtypeStruct(x.shape, f32) for x in (xi_coarse, xi_middle, xi_fine)]
    *grads, total = pl.pallas_call(
        functools.partial(kernel, m, n, cells),
        name="prior_gradient",
        out_shape=(*shapes, jax.ShapeDtypeStruct((1, 1), f32)),
        in_specs=[hbm] * 11,
        out_specs=[hbm] * 4,
        scratch_shapes=scratch,
        compiler_params=pltpu.CompilerParams(
            collective_id=0, has_side_effects=True, vmem_limit_bytes=62 * 1024 * 1024
        ),
    )(
        xi_coarse, xi_middle, xi_fine, coef_middle, coef_fine, kern_u, kern_v, vis_data,
        facet_tiles, facet_weight, facet_count,
    )
    grads = pl.pallas_call(
        finish,
        name="hand_out",
        out_shape=shapes,
        in_specs=[hbm] * 3,
        out_specs=[hbm] * 3,
        scratch_shapes=[*[vmem(s.shape, f32) for s in shapes], dma((8,)), dma((8,))],
    )(*grads)
    return (*grads, total.reshape(()))


def solution(mesh):
    placed = (
        P("gx", "gy"),
        P("gx", "gy"),
        P("gx", "gy"),
        P(None, None, "gx", "gy"),
        P(None, None, "gx", "gy"),
        P("gx", "gy", None, None),
        P("gx", "gy", None, None),
        P("gx", "gy", None, None),
        P("gx", "gy", None),
        P("gx", "gy", None),
        P("gx", "gy"),
    )
    return jax.shard_map(
        body,
        mesh=mesh,
        in_specs=placed,
        out_specs=(P("gx", "gy"), P("gx", "gy"), P("gx", "gy"), P()),
        check_vma=False,
    )
```

```python
import functools

import jax
import jax.numpy as jnp
from jax import lax
from jax.experimental import pallas as pl
from jax.experimental.pallas import tpu as pltpu
from jax.sharding import PartitionSpec as P

inv_noise = 0.125
MESH = pl.DeviceIdType.MESH
ROW, LANE = 8, 128
END = 16
SIDES = [(dx, dy) for dx in (-1, 0, 1) for dy in (-1, 0, 1) if (dx, dy) != (0, 0)]


def f32dot(a, b, contract):
    return lax.dot_general(a, b, ((contract[:1], contract[1:]), ((), ())), preferred_element_type=jnp.float32)


def split(x):
    high = x.astype(jnp.bfloat16)
    return high, (x - high.astype(jnp.float32)).astype(jnp.bfloat16)


def strip(side, size, edge, near):
    if side == 0:
        return edge, size
    if near:
        return (edge, edge) if side < 0 else (size, edge)
    return (0, edge) if side < 0 else (edge + size, edge)


def diagonal():
    row = lax.broadcasted_iota(jnp.int32, (LANE, LANE), 0)
    return row == lax.broadcasted_iota(jnp.int32, (LANE, LANE), 1)


class Halo:
    def __init__(self, src, rows_in, cols_out, cols_in, near, send, recv, at):
        gx, gy, m, n = at
        self.src, self.rows_in, self.cols_out, self.cols_in, self.near, self.at = src, rows_in, cols_out, cols_in, near, at
        self.size = size = src.shape[0] - 2 * ROW
        self.copies = []
        for i, (dx, dy) in enumerate(SIDES):
            side = 0 if max(dx, -1) > 0 or (dx == 0 and dy > 0) else 1
            if dx:
                source = src.at[pl.ds(*strip(dx, size, ROW, near)), pl.ds(*strip(dy, size, LANE, near))]
                target = rows_in.at[side, :, pl.ds(*strip(-dy, size, LANE, False))]
            else:
                source, target = cols_out.at[side], cols_in.at[side]
            self.copies.append(
                pltpu.make_async_remote_copy(
                    src_ref=source,
                    dst_ref=target,
                    send_sem=send.at[i],
                    recv_sem=recv.at[i],
                    device_id=(lax.rem(gx + dx + m, m), lax.rem(gy + dy + n, n)),
                    device_id_type=MESH,
                )
            )

    def start(self):
        self.pack()
        self.send()

    def pack(self):
        size, eye = self.size, diagonal()
        for side, dy in ((0, 1), (1, -1)):
            lane = (LANE + size - 1 if dy > 0 else LANE) if self.near else (LANE + size if dy > 0 else LANE - 1)
            tile = lane // LANE * LANE
            for b in range(size // LANE):
                block = self.src[ROW + b * LANE : ROW + (b + 1) * LANE, tile : tile + LANE]
                block = jnp.broadcast_to(block[:, lane - tile : lane - tile + 1], (LANE, LANE))
                self.cols_out[side, b : b + 1, :] = jnp.sum(jnp.where(eye, block, 0.0), axis=0, keepdims=True)

    def send(self):
        for c in self.copies:
            c.start()

    def wait(self):
        for c in self.copies:
            c.wait()

    def column(self, side):
        gx, gy, m, n = self.at
        inside = gy > 0 if side == 0 else gy < n - 1
        blocks = []
        for b in range(self.size // LANE):
            block = jnp.broadcast_to(self.cols_in[side, b : b + 1, :], (LANE, LANE))
            blocks.append(jnp.sum(jnp.where(diagonal(), block, 0.0), axis=1, keepdims=True))
        return jnp.where(inside, jnp.concatenate(blocks, axis=0), 0.0)

    def strips(self, side):
        gx, gy, m, n = self.at
        inside = gx > 0 if side == 0 else gx < m - 1
        value = jnp.where(inside, self.rows_in[side], 0.0)
        left, right = value[:, 0:LANE], value[:, LANE + self.size : 2 * LANE + self.size]
        return jnp.where(gy > 0, left, 0.0), value[:, LANE : LANE + self.size], jnp.where(gy < n - 1, right, 0.0)

    def surround(self, pad):
        size = self.size
        for side, start in ((0, 0), (1, ROW + size)):
            before, middle, after = self.strips(side)
            before = jnp.broadcast_to(before[:, LANE - 1 : LANE], (ROW, LANE))
            after = jnp.broadcast_to(after[:, 0:1], (ROW, LANE))
            pad[start : start + ROW, :] = jnp.concatenate([before, middle, after], axis=1)
        for side, start in ((0, 0), (1, LANE + size)):
            pad[ROW : ROW + size, start : start + LANE] = jnp.broadcast_to(self.column(side), (size, LANE))

    def fold(self, result):
        size = self.size
        first, last = slice(LANE, 2 * LANE), slice(size, size + LANE)
        for side, rows in ((0, slice(ROW, 2 * ROW)), (1, slice(size, size + ROW))):
            left, middle, right = self.strips(side)
            result[rows, LANE : LANE + size] += middle
            result[rows, first] += left
            result[rows, last] += right
        lane = lax.broadcasted_iota(jnp.int32, (size, LANE), 1)
        full = slice(ROW, ROW + size)
        result[full, first] += jnp.where(lane == 0, self.column(0), 0.0)
        result[full, last] += jnp.where(lane == LANE - 1, self.column(1), 0.0)


class Exchange:
    def __init__(self, src, dst, send, recv, at, slab, cols=None):
        self.src, self.dst, self.send, self.recv, self.at, self.slab = src, dst, send, recv, at, slab
        self.cols = slice(0, src.shape[1]) if cols is None else cols

    def rows(self, index):
        return pl.ds(pl.multiple_of(index * self.slab, self.slab), self.slab)

    def copy(self, k):
        gx, gy, m, n = self.at
        peer = lax.rem(gy + k, n)
        return pltpu.make_async_remote_copy(
            src_ref=self.src.at[self.rows(peer), self.cols],
            dst_ref=self.dst.at[self.rows(gy), self.cols],
            send_sem=self.send.at[k],
            recv_sem=self.recv.at[k],
            device_id=(gx, peer),
            device_id_type=MESH,
        )

    def own(self):
        here = self.rows(self.at[1])
        self.dst[here, self.cols] = self.src[here, self.cols]

    def start(self):
        @pl.loop(1, self.at[3])
        def _(k):
            self.copy(k).start()

        self.own()

    def wait(self):
        @pl.loop(1, self.at[3])
        def _(k):
            self.copy(k).wait()

    def start_ends(self):
        gy, n = self.at[1], self.at[3]
        self.own()
        for ends in (True, False):

            @pl.loop(1, n)
            def _(k):
                peer = lax.rem(gy + k, n)
                at_end = (peer == 0) | (peer == n - 1)

                @pl.when(at_end if ends else jnp.logical_not(at_end))
                def _():
                    self.copy(k).start()


def spread(ref):
    size = ref.shape[0]
    half = size // 2
    row = lax.broadcasted_iota(jnp.int32, (half, size), 0)
    col = lax.broadcasted_iota(jnp.int32, (half, size), 1)
    ref[0:half, :] = jnp.where(col == 2 * row, 1.0, 0.0).astype(jnp.bfloat16)
    ref[half:size, :] = jnp.where(col == 2 * row + 1, 1.0, 0.0).astype(jnp.bfloat16)


def refine(pad, wins, coef, rolled, high, low, size, rows):
    own = pad[:, LANE : LANE + size]
    lane = lax.broadcasted_iota(jnp.int32, own.shape, 1)
    for dj in (-1, 0, 1):
        value = own
        if dj:
            beyond = pad[:, 0:LANE] if dj < 0 else pad[:, LANE + size : 2 * LANE + size]
            beyond = jnp.concatenate([beyond] * (size // LANE), axis=1)
            value = jnp.where(lane == (0 if dj < 0 else size - 1), beyond, pltpu.roll(own, (-dj) % size, 1))
        rolled[...] = value
        for di in (-1, 0, 1):
            wins[3 * (di + 1) + dj + 1] = rolled[ROW + di : ROW + di + size, :]

    @pl.loop(0, size // rows)
    def _(step):
        at = pl.multiple_of(step * rows, rows)
        here = pl.ds(at, rows)
        totals = [None] * 4
        for near in range(9):
            window = wins[near, here, :]
            for child in range(4):
                term = coef[child, near, here, :].astype(jnp.float32) * window
                totals[child] = term if near == 0 else totals[child] + term
        for child in range(4):
            a, b = child // 2, child % 2
            there = pl.ds(pl.multiple_of(a * size + at, rows), rows)
            high[there, b * size : (b + 1) * size], low[there, b * size : (b + 1) * size] = split(totals[child])


def interleave(high, low, matrix, laced, size):
    for a in (0, 1):
        rows = slice(a * size, (a + 1) * size)
        value = f32dot(high[rows, :], matrix[...], (1, 0)) + f32dot(low[rows, :], matrix[...], (1, 0))
        for c in range(2 * size // LANE):
            laced[c, pl.ds(a, size, stride=2), :] = value[:, c * LANE : (c + 1) * LANE]


def parent_terms(quads, coef, shifted, result, size, rows):
    width = size + 2 * LANE
    tall = size + 4 * ROW
    for d in range(3):
        shifted[d, 0 : 2 * ROW, :] = jnp.zeros((2 * ROW, width), jnp.float32)
        shifted[d, tall - 2 * ROW : tall, :] = jnp.zeros((2 * ROW, width), jnp.float32)

    @pl.loop(0, size // rows)
    def _(step):
        at = pl.multiple_of(step * rows, rows)
        here = pl.ds(at, rows)
        quad = [
            quads[pl.ds(pl.multiple_of(a * size + at, rows), rows), b * size : (b + 1) * size]
            for a in (0, 1)
            for b in (0, 1)
        ]
        lane = lax.broadcasted_iota(jnp.int32, (rows, size), 1)
        for d in range(3):
            parts = []
            for j in range(3):
                part = None
                for child in range(4):
                    term = coef[child, 3 * d + j, here, :].astype(jnp.float32) * quad[child]
                    part = term if child == 0 else part + term
                parts.append(part if j == 1 else pltpu.roll(part, (j - 1) % size, 1))
            total = parts[1] + jnp.where(lane < size - 1, parts[0], 0.0) + jnp.where(lane > 0, parts[2], 0.0)
            before = jnp.where(lane == size - 1, parts[0], 0.0)[:, size - LANE : size]
            after = jnp.where(lane == 0, parts[2], 0.0)[:, 0:LANE]
            total = jnp.concatenate([before, total, after], axis=1)
            shifted[d, pl.ds(pl.multiple_of(at + 2 * ROW, ROW), rows), :] = total

    high = tall - 2 * ROW
    result[...] = (
        shifted[1, ROW : ROW + high, :]
        + shifted[2, ROW - 1 : ROW - 1 + high, :]
        + shifted[0, ROW + 1 : ROW + 1 + high, :]
    )


def rim_terms(quads, coef, shifted, result, size, rows):
    width = size + 2 * LANE
    tall = size + 4 * ROW
    for d in range(3):
        shifted[d, 0 : 2 * ROW, :] = jnp.zeros((2 * ROW, width), jnp.float32)
        shifted[d, tall - 2 * ROW : tall, :] = jnp.zeros((2 * ROW, width), jnp.float32)

    def term(near, at, start, length):
        here = pl.ds(at, rows)
        total = None
        for child in range(4):
            row = pl.ds(pl.multiple_of(child // 2 * size + at, rows), rows)
            column = child % 2 * size + start
            part = coef[child, near, here, start : start + length].astype(jnp.float32) * quads[row, column : column + length]
            total = part if child == 0 else total + part
        return total

    @pl.loop(0, size // rows)
    def _(step):
        at = pl.multiple_of(step * rows, rows)
        lane = lax.broadcasted_iota(jnp.int32, (rows, LANE), 1)
        for d in range(3):
            for j, start, edge, put in ((0, 0, 0, 0), (2, size - LANE, LANE - 1, LANE + size)):
                part = jnp.where(lane == edge, term(3 * d + j, at, start, LANE), 0.0)
                shifted[d, pl.ds(pl.multiple_of(at + 2 * ROW, ROW), rows), put : put + LANE] = pltpu.roll(
                    part, (j - 1) % LANE, 1
                )

    lane = lax.broadcasted_iota(jnp.int32, (rows, size), 1)
    for d, at in ((0, 0), (2, size - rows)):
        before = pltpu.roll(term(3 * d, at, 0, size), size - 1, 1)
        after = pltpu.roll(term(3 * d + 2, at, 0, size), 1, 1)
        total = term(3 * d + 1, at, 0, size) + jnp.where(lane < size - 1, before, 0.0) + jnp.where(lane > 0, after, 0.0)
        shifted[d, at + 2 * ROW : at + 2 * ROW + rows, LANE : LANE + size] = total

    def summed(start, length, cols):
        at = start + ROW
        return (
            shifted[1, at : at + length, cols]
            + shifted[2, at - 1 : at - 1 + length, cols]
            + shifted[0, at + 1 : at + 1 + length, cols]
        )

    for start in (0, ROW + size):
        result[start : start + ROW, :] = summed(start, ROW, slice(0, width))
    for start in (0, LANE + size):
        cols = slice(start, start + LANE)
        result[ROW : ROW + size, cols] = summed(ROW, size, cols)


def squares(x):
    return jnp.sum(x * x, axis=0, keepdims=True)


def fold_lanes(x):
    total = x[:, 0:LANE]
    for c in range(1, x.shape[1] // LANE):
        total = total + x[:, c * LANE : (c + 1) * LANE]
    return total


def kernel(
    m, n, cells,
    xi_c, xi_m, xi_f, co_m, co_f, k_u, k_v, v_d, f_t, f_w, f_c,
    g_c, g_m, g_f, pot,
    pad_c, pad_m, xm, xf, cm, cf, ku, kv, vd, kut,
    roll_c, roll_m, win_c, win_m, hi_c, lo_c, hi_m, lo_m, lace_c, lace_m, mat_c, mat_m,
    listed, weights, counts, total_s, meta, metas, mix_hi, mix_lo, sky, sky_2, edge, edges, late, lates, tiles, tiles_o, sums, fsum, damps, dsum, dslab, back_b, dsky, dtile, ends,
    quad_c, quad_m, shift_c, shift_m, res_c, res_m, res_r, grad_c, grad_m, grad_f, back_v,
    row_c, row_m, row_f, row_b, col_o, col_i,
    parts, part_y, part_x,
    load, few, save, sem_s, sem_r, a2a_s, a2a_r, sem_ls, sem_lr, sem_es, sem_er, sem_ts, sem_tr, sem_ys, sem_yr, sem_xs, sem_xr,
):
    gx, gy = lax.axis_index("gx"), lax.axis_index("gy")
    at = (gx, gy, m, n)
    nc, nm, nf = xi_c.shape[0], xi_m.shape[0], xi_f.shape[0]
    slab = nf // n
    facets = k_u.shape[1]
    bins = v_d.shape[2]

    barrier = pltpu.get_barrier_semaphore()
    greeted = 0
    for dx in (-1, 1):
        for dy in (-1, 1):
            pl.semaphore_signal(
                barrier, inc=1, device_id=(lax.rem(gx + dx + m, m), lax.rem(gy + dy + n, n)), device_id_type=MESH
            )
            greeted += 1
    for k in range(1, m):
        pl.semaphore_signal(barrier, inc=1, device_id=(lax.rem(gx + k, m), gy), device_id_type=MESH)
        greeted += 1
    for k in range(1, n):
        pl.semaphore_signal(barrier, inc=1, device_id=(gx, lax.rem(gy + k, n)), device_id_type=MESH)
        greeted += 1

    left, right, inside = slice(0, LANE), slice(nf - LANE, nf), slice(LANE, nf - LANE)
    halves = (slice(0, 2 * LANE), slice(2 * LANE, nf))
    moved = ((left, slice(0, LANE)), (right, slice(LANE, 2 * LANE)), (inside, halves[1]))
    small = [
        pltpu.make_async_copy(src, dst, few.at[i])
        for i, (src, dst) in enumerate(((f_t, listed), (f_w, weights), (f_c, counts)))
    ]
    loads = [
        pltpu.make_async_copy(src, dst, load.at[i])
        for i, (src, dst) in enumerate(
            (
                (xi_c, pad_c.at[ROW : ROW + nc, LANE : LANE + nc]),
                (co_m, cm),
                (xi_m, xm),
                (co_f, cf),
                (xi_f, xf),
                (k_u.at[0], ku),
                *((k_v.at[0, :, :, natural], kv.at[:, :, put]) for natural, put in moved),
                (v_d.at[0], vd),
            )
        )
    ]
    for c in loads[:3] + small + loads[3:]:
        c.start()

    def blank(pad, size):
        width = size + 2 * LANE
        pad[0:ROW, :] = jnp.zeros((ROW, width), jnp.float32)
        pad[ROW + size : 2 * ROW + size, :] = jnp.zeros((ROW, width), jnp.float32)
        pad[ROW : ROW + size, 0:LANE] = jnp.zeros((size, LANE), jnp.float32)
        pad[ROW : ROW + size, LANE + size : width] = jnp.zeros((size, LANE), jnp.float32)

    def middle_level():
        refine(pad_c, win_c, cm, roll_c, hi_c, lo_c, nc, 32)
        interleave(hi_c, lo_c, mat_c, lace_c, nc)
        for c in range(nm // LANE):
            cols = slice(c * LANE, (c + 1) * LANE)
            pad_m[ROW : ROW + nm, LANE + c * LANE : LANE + (c + 1) * LANE] = lace_c[c] + xm[:, cols]

    def fine_level(out):
        refine(pad_m, win_m, cf, roll_m, hi_m, lo_m, nm, 16)
        interleave(hi_m, lo_m, mat_m, lace_m, nm)
        for c in range(nf // LANE):
            cols = slice(c * LANE, (c + 1) * LANE)
            out[:, cols] = (lace_m[c] + xf[:, cols]).astype(jnp.bfloat16)

    def halo(i, src, rows_in, near):
        return Halo(src, rows_in, col_o.at[i], col_i.at[i], near, sem_s.at[i], sem_r.at[i], at)

    def exchange(i, src, dst, cols=None):
        return Exchange(src, dst, a2a_s.at[i], a2a_r.at[i], at, slab, cols)

    spread(mat_c)
    spread(mat_m)
    blank(pad_c, nc)
    blank(pad_m, nm)
    for c in small:
        c.wait()
    for f in range(facets):
        for s in range(2):
            i = 2 * f + s
            meta[i : i + 1, :] = jnp.full((1, LANE), listed[0, f, s].astype(jnp.float32))
            meta[4 + i : 5 + i, :] = jnp.full((1, LANE), weights[0, f, s])
    col_o[...] = jnp.zeros_like(col_o)
    loads[0].wait()
    halo_c = halo(0, pad_c, row_c, True)
    halo_c.pack()
    pl.semaphore_wait(barrier, greeted)
    halo_c.send()

    def meta_copy(k):
        return pltpu.make_async_remote_copy(
            src_ref=meta,
            dst_ref=metas.at[gy],
            send_sem=sem_ts.at[k],
            recv_sem=sem_tr.at[k],
            device_id=(gx, lax.rem(gy + k, n)),
            device_id_type=MESH,
        )

    @pl.loop(1, n)
    def _(k):
        meta_copy(k).start()

    metas[gy] = meta[...]
    for c in loads[1:3]:
        c.wait()
    middle_level()
    for c in loads[3:5]:
        c.wait()
    fine_level(sky)
    early = exchange(0, sky, tiles)

    halo_c.wait()
    halo_c.surround(pad_c)
    middle_level()
    halo_m = halo(1, pad_m, row_m, True)
    halo_m.start()
    early.start()

    @pl.loop(1, n)
    def _(k):
        meta_copy(k).wait()

    lane = lax.broadcasted_iota(jnp.int32, (slab, nf), 1)
    row = lax.broadcasted_iota(jnp.int32, (slab, nf), 0)
    tile_of = (lane // slab).astype(jnp.float32)
    same = lane % slab == row

    @pl.loop(0, n)
    def _(o):
        rows = pl.ds(pl.multiple_of(o * slab, slab), slab)
        value = metas[o]
        for f in range(facets):
            total = jnp.zeros((slab, nf), jnp.float32)
            for s in range(2):
                i = 2 * f + s
                tile = jnp.concatenate([value[i : i + 1, :]] * (nf // LANE), axis=1)
                weight = jnp.concatenate([value[4 + i : 5 + i, :]] * (nf // LANE), axis=1)
                total = total + jnp.where((tile == tile_of) & same, weight, 0.0)
            mix_hi[f, rows, :], mix_lo[f, rows, :] = split(total)

    owners = ((0, 0), (1, n - 1))

    def late_copy(e, owner, source):
        return pltpu.make_async_remote_copy(
            src_ref=late.at[e],
            dst_ref=lates.at[source],
            send_sem=sem_ls.at[e],
            recv_sem=sem_lr.at[source],
            device_id=(gx, owner),
            device_id_type=MESH,
        )

    halo_m.wait()
    halo_m.surround(pad_m)
    fine_level(sky_2)
    outer = lax.broadcasted_iota(jnp.int32, (nf, LANE), 1) < LANE // 2
    edge[...] = jnp.where(outer, sky_2[:, left], sky_2[:, right])
    rim = exchange(1, edge, edges)
    for e, owner in owners:
        start = owner * slab + e * (slab - END)
        rows = sky_2[start : start + END, :].astype(jnp.float32)[e * ROW : (e + 1) * ROW, :]
        late[e] = jnp.concatenate([rows[:, 0 : nf // 2], rows[:, nf // 2 : nf]], axis=0).astype(jnp.bfloat16)

        @pl.when(gy != owner)
        def _(e=e, owner=owner):
            late_copy(e, owner, gy).start()

        @pl.when(gy == owner)
        def _(e=e, owner=owner):
            lates[owner] = late[e]

    rim.start()

    prior = fold_lanes(squares(pad_c[ROW : ROW + nc, LANE : LANE + nc]))
    prior = prior + fold_lanes(squares(xm[...])) + fold_lanes(squares(xf[...]))
    parts[...] = jnp.zeros_like(parts)
    early.wait()
    for e, owner in owners:

        @pl.when(gy != owner)
        def _(e=e, owner=owner):
            late_copy(e, owner, gy).wait_send()

        @pl.when(gy == owner)
        def _(e=e, owner=owner):
            @pl.loop(1, n)
            def _(k):
                late_copy(e, owner, lax.rem(owner + k, n)).wait_recv()

            for i in range(n):
                at_row = i * slab + e * (slab - END)
                new = lates[i].astype(jnp.float32)
                new = jnp.concatenate([new[0:ROW, :], new[ROW : 2 * ROW, :]], axis=1)
                old = tiles[at_row : at_row + END, :].astype(jnp.float32)
                pair = [old[0:ROW, :], new] if e else [new, old[ROW:END, :]]
                tiles[at_row : at_row + END, :] = jnp.concatenate(pair, axis=0).astype(jnp.bfloat16)

    rim.wait()
    mixed = jnp.concatenate(
        [jnp.where(outer, edges[...], tiles[:, left]), jnp.where(outer, tiles[:, right], edges[...]), tiles[:, inside]],
        axis=1,
    )
    tiles_o[...] = mixed
    out = []
    for f in range(facets):
        sums[f] = (f32dot(mix_hi[f], tiles_o[...], (1, 0)) + f32dot(mix_lo[f], tiles_o[...], (1, 0))).astype(jnp.bfloat16)
        out.append(exchange(2 + f, sums.at[f], fsum.at[f]))
        out[f].start()

    for c in loads[5:]:
        c.wait()
    for f in range(facets):
        kut[f] = ku[f].T
    home = []
    chunk = 512
    for f in range(facets):
        out[f].wait()
        count = counts[0, f]

        for step in range(bins // chunk):
            here = slice(step * chunk, (step + 1) * chunk)
            amp = f32dot(ku[f, here, :], fsum[f], (1, 0)).astype(jnp.bfloat16)
            vis = f32dot(amp, kv[f], (1, 1))
            bin_at = step * chunk + lax.broadcasted_iota(jnp.int32, (chunk, bins), 0)
            resid = jnp.where(bin_at < count, vis - vd[f, here, :].astype(jnp.float32), 0.0)
            parts[...] += squares(resid)
            dvis = (inv_noise * resid).astype(jnp.bfloat16)
            damps[here, :] = f32dot(dvis, kv[f], (1, 0)).astype(jnp.bfloat16)

        for h, cols in enumerate(halves):
            dsum[f, :, cols] = f32dot(kut[f], damps[:, cols], (1, 0)).astype(jnp.bfloat16)
            going = exchange(2 + facets + 2 * f + h, dsum.at[f], dslab.at[f], cols)
            home.append(going)
            if f < facets - 1 or h == 0:
                going.start()
            else:
                going.start_ends()

    own = 0.5 * prior + 0.5 * inv_noise * fold_lanes(parts[...])
    part_y[gy] = jnp.where(lax.broadcasted_iota(jnp.int32, (ROW, LANE), 0) == 0, own, 0.0)

    def pot_y(k):
        return pltpu.make_async_remote_copy(
            src_ref=part_y.at[gy],
            dst_ref=part_y.at[gy],
            send_sem=sem_ys.at[k],
            recv_sem=sem_yr.at[k],
            device_id=(gx, lax.rem(gy + k, n)),
            device_id_type=MESH,
        )

    def pot_x(k):
        return pltpu.make_async_remote_copy(
            src_ref=part_x.at[gx],
            dst_ref=part_x.at[gx],
            send_sem=sem_xs.at[k],
            recv_sem=sem_xr.at[k],
            device_id=(lax.rem(gx + k, m), gy),
            device_id_type=MESH,
        )

    @pl.loop(1, n)
    def _(k):
        pot_y(k).start()

    def unmix(f, cols):
        return f32dot(mix_hi[f], dslab[f, :, cols], (0, 0)) + f32dot(mix_lo[f], dslab[f, :, cols], (0, 0))

    for f in range(facets - 1):
        for h, cols in enumerate(halves):
            home[2 * f + h].wait()
            part = unmix(f, cols)
            back_v[:, cols] = part if f == 0 else back_v[:, cols] + part
    def ends_copy(e, k):
        peer = lax.rem(gy + k, n)
        return pltpu.make_async_remote_copy(
            src_ref=back_b.at[ends_rows(e, peer), halves[1]],
            dst_ref=ends.at[e],
            send_sem=sem_es.at[e, k],
            recv_sem=sem_er.at[e, k],
            device_id=(gx, peer),
            device_id_type=MESH,
        )

    def ends_rows(e, index):
        return pl.ds(pl.multiple_of(index * slab + e * (slab - END), END), END)

    def ends_start():
        for e, owner in owners:

            @pl.when(gy == owner)
            def _(e=e):
                @pl.loop(1, n)
                def _(k):
                    ends_copy(e, k).start()

                ends[e] = back_b[ends_rows(e, gy), halves[1]]

    def ends_wait():
        for e, owner in owners:

            @pl.when(gy == owner)
            def _(e=e):
                @pl.loop(1, n)
                def _(k):
                    ends_copy(e, k).wait_send()

            @pl.when(gy != owner)
            def _(e=e, owner=owner):
                ends_copy(e, lax.rem(gy - owner + n, n)).wait_recv()

    last = []
    f = facets - 1
    for h, cols in enumerate(halves):
        home[2 * f + h].wait()
        part = unmix(f, cols)
        back_b[:, cols] = (back_v[:, cols] + part if f else part).astype(jnp.bfloat16)
        if h:
            ends_start()
        last.append(exchange(2 + 3 * facets + h, back_b, dsky, cols))
        last[h].start()

    @pl.loop(1, n)
    def _(k):
        pot_y(k).wait()

    part_x[gx] = jnp.sum(part_y[...], axis=0)

    @pl.loop(1, m)
    def _(k):
        pot_x(k).start()

    def adjoint_fine(terms, result):
        for a in (0, 1):
            rows = slice(a * nm, (a + 1) * nm)
            lined = f32dot(mat_m[rows, :], dtile[...], (1, 0)).astype(jnp.bfloat16)
            quad_m[rows, :] = f32dot(lined, mat_m[...], (1, 1))
        terms(quad_m, cf, shift_m, result, nm, 16)

    last[0].wait()
    dtile[:, left] = dsky[:, 0:LANE]
    dtile[:, right] = dsky[:, LANE : 2 * LANE]
    dtile[END : nf - END, inside] = jnp.zeros((nf - 2 * END, nf - 2 * LANE), jnp.bfloat16)
    ends_wait()
    dtile[0:END, inside] = ends[0]
    dtile[nf - END : nf, inside] = ends[1]
    adjoint_fine(rim_terms, res_r)
    halo_f = halo(2, res_r, row_f, False)
    halo_f.start()
    last[1].wait()
    dtile[:, inside] = dsky[:, halves[1]]
    adjoint_fine(parent_terms, res_m)
    grad_f[...] = dtile[...].astype(jnp.float32) + xf[...]
    save_f = pltpu.make_async_copy(grad_f, g_f, save.at[0])
    save_f.start()
    halo_f.wait()
    halo_f.fold(res_m)
    dmiddle = res_m[ROW : ROW + nm, LANE : LANE + nm]
    high, low = split(dmiddle)
    for a in (0, 1):
        rows = slice(a * nc, (a + 1) * nc)
        matrix = mat_c[rows, :]
        quad_c[rows, :] = f32dot(
            f32dot(matrix, high, (1, 0)).astype(jnp.bfloat16), mat_c[...], (1, 1)
        ) + f32dot(f32dot(matrix, low, (1, 0)).astype(jnp.bfloat16), mat_c[...], (1, 1))
    parent_terms(quad_c, cm, shift_c, res_c, nc, 32)
    halo_b = halo(3, res_c, row_b, False)
    halo_b.start()
    grad_m[...] = res_m[ROW : ROW + nm, LANE : LANE + nm] + xm[...]
    save_m = pltpu.make_async_copy(grad_m, g_m, save.at[1])
    save_m.start()

    @pl.loop(1, m)
    def _(k):
        pot_x(k).wait()

    total_s[0, 0] = jnp.sum(part_x[...]) / cells
    save_p = pltpu.make_async_copy(total_s, pot, save.at[3])
    save_p.start()
    halo_b.wait()
    halo_b.fold(res_c)
    grad_c[...] = res_c[ROW : ROW + nc, LANE : LANE + nc] + pad_c[ROW : ROW + nc, LANE : LANE + nc]
    save_c = pltpu.make_async_copy(grad_c, g_c, save.at[2])
    save_c.start()
    save_f.wait()
    save_m.wait()
    save_c.wait()
    save_p.wait()


def finish(*refs):
    count = (len(refs) - 2) // 3
    given, given_out, held = refs[:count], refs[count : 2 * count], refs[2 * count : 3 * count]
    come, go = refs[3 * count :]
    blocks = []
    for a, b, v in zip(given, given_out, held):
        rows = min(LANE, a.shape[0])
        for start in range(0, a.shape[0], rows):
            here = slice(start, start + rows)
            i = len(blocks)
            blocks.append(
                (
                    pltpu.make_async_copy(a.at[here, :], v.at[here, :], come.at[i]),
                    pltpu.make_async_copy(v.at[here, :], b.at[here, :], go.at[i]),
                )
            )
    for read, _ in blocks:
        read.start()
    for read, write in blocks:
        read.wait()
        write.start()
    for _, write in blocks:
        write.wait()


def body(
    xi_coarse, xi_middle, xi_fine, coef_middle, coef_fine, kern_u, kern_v, vis_data, facet_tiles, facet_weight, facet_count
):
    m, n = lax.axis_size("gx"), lax.axis_size("gy")
    nc, nm, nf = xi_coarse.shape[0], xi_middle.shape[0], xi_fine.shape[0]
    facets, bins = kern_u.shape[1], vis_data.shape[2]
    cells = float(m * n * nf * nf)
    f32, bf16 = jnp.float32, jnp.bfloat16
    vmem, dma = pltpu.VMEM, pltpu.SemaphoreType.DMA

    def wide(size):
        return vmem((size + 2 * ROW, size + 2 * LANE), f32)

    def strips(size):
        return vmem((2, ROW, size + 2 * LANE), f32)

    swaps = 4 + 3 * facets
    scratch = [
        wide(nc), wide(nm), vmem((nm, nm), f32), vmem((nf, nf), f32),
        vmem(coef_middle.shape, bf16), vmem(coef_fine.shape, bf16),
        vmem(kern_u.shape[1:], bf16), vmem(kern_v.shape[1:], bf16), vmem(vis_data.shape[1:], bf16),
        vmem((facets, nf, bins), bf16),
        vmem((nc + 2 * ROW, nc), f32), vmem((nm + 2 * ROW, nm), f32),
        vmem((9, nc, nc), f32), vmem((9, nm, nm), f32),
        vmem((nm, nm), bf16), vmem((nm, nm), bf16), vmem((nf, nf), bf16), vmem((nf, nf), bf16),
        vmem((nm // LANE, nm, LANE), f32), vmem((nf // LANE, nf, LANE), f32),
        vmem((nm, nm), bf16), vmem((nf, nf), bf16),
        pltpu.SMEM(facet_tiles.shape, jnp.int32), pltpu.SMEM(facet_weight.shape, f32),
        pltpu.SMEM(facet_count.shape, jnp.int32), pltpu.SMEM((1, 1), f32),
        vmem((8, LANE), f32), vmem((n, 8, LANE), f32), vmem((facets, nf, nf), bf16), vmem((facets, nf, nf), bf16),
        vmem((nf, nf), bf16), vmem((nf, nf), bf16), vmem((nf, LANE), bf16), vmem((nf, LANE), bf16),
        vmem((2, END, nf // 2), bf16), vmem((n, END, nf // 2), bf16), vmem((nf, nf), bf16), vmem((nf, nf), bf16),
        vmem((facets, nf, nf), bf16), vmem((facets, nf, nf), bf16),
        vmem((bins, nf), bf16), vmem((facets, nf, nf), bf16), vmem((facets, nf, nf), bf16),
        vmem((nf, nf), bf16), vmem((nf, nf), bf16), vmem((nf, nf), bf16), vmem((2, END, nf - 2 * LANE), bf16),
        vmem((nm, nm), f32), vmem((nf, nf), f32),
        vmem((3, nc + 4 * ROW, nc + 2 * LANE), f32), vmem((3, nm + 4 * ROW, nm + 2 * LANE), f32),
        wide(nc), wide(nm), wide(nm), vmem((nc, nc), f32), vmem((nm, nm), f32), vmem((nf, nf), f32), vmem((nf, nf), f32),
        strips(nc), strips(nm), strips(nm), strips(nc), vmem((4, 2, ROW, LANE), f32), vmem((4, 2, ROW, LANE), f32),
        vmem((1, bins), f32), vmem((n, 8, LANE), f32), vmem((m, 8, LANE), f32),
        dma((10,)), dma((3,)), dma((4,)), dma((4, 8)), dma((4, 8)),
        dma((swaps, n)), dma((swaps, n)), dma((2,)), dma((n,)), dma((2, n)), dma((2, n)),
        dma((n,)), dma((n,)), dma((n,)), dma((n,)), dma((m,)), dma((m,)),
    ]
    hbm = pl.BlockSpec(memory_space=pl.ANY)
    shapes = [jax.ShapeDtypeStruct(x.shape, f32) for x in (xi_coarse, xi_middle, xi_fine)]
    *grads, total = pl.pallas_call(
        functools.partial(kernel, m, n, cells),
        name="prior_gradient",
        out_shape=(*shapes, jax.ShapeDtypeStruct((1, 1), f32)),
        in_specs=[hbm] * 11,
        out_specs=[hbm] * 4,
        scratch_shapes=scratch,
        compiler_params=pltpu.CompilerParams(
            collective_id=0, has_side_effects=True, vmem_limit_bytes=62 * 1024 * 1024
        ),
    )(
        xi_coarse, xi_middle, xi_fine, coef_middle, coef_fine, kern_u, kern_v, vis_data,
        facet_tiles, facet_weight, facet_count,
    )
    grads = pl.pallas_call(
        finish,
        name="hand_out",
        out_shape=shapes,
        in_specs=[hbm] * 3,
        out_specs=[hbm] * 3,
        scratch_shapes=[*[vmem(s.shape, f32) for s in shapes], dma((8,)), dma((8,))],
    )(*grads)
    return (*grads, total.reshape(()))


def solution(mesh):
    placed = (
        P("gx", "gy"),
        P("gx", "gy"),
        P("gx", "gy"),
        P(None, None, "gx", "gy"),
        P(None, None, "gx", "gy"),
        P("gx", "gy", None, None),
        P("gx", "gy", None, None),
        P("gx", "gy", None, None),
        P("gx", "gy", None),
        P("gx", "gy", None),
        P("gx", "gy"),
    )
    return jax.shard_map(
        body,
        mesh=mesh,
        in_specs=placed,
        out_specs=(P("gx", "gy"), P("gx", "gy"), P("gx", "gy"), P()),
        check_vma=False,
    )
```

```python
import functools

import jax
import jax.numpy as jnp
from jax import lax
from jax.experimental import pallas as pl
from jax.experimental.pallas import tpu as pltpu
from jax.sharding import PartitionSpec as P

inv_noise = 0.125
MESH = pl.DeviceIdType.MESH
ROW, LANE = 8, 128
END = 16
SIDES = [(dx, dy) for dx in (-1, 0, 1) for dy in (-1, 0, 1) if (dx, dy) != (0, 0)]


def f32dot(a, b, contract):
    return lax.dot_general(a, b, ((contract[:1], contract[1:]), ((), ())), preferred_element_type=jnp.float32)


def split(x):
    high = x.astype(jnp.bfloat16)
    return high, (x - high.astype(jnp.float32)).astype(jnp.bfloat16)


def strip(side, size, edge, near):
    if side == 0:
        return edge, size
    if near:
        return (edge, edge) if side < 0 else (size, edge)
    return (0, edge) if side < 0 else (edge + size, edge)


def diagonal():
    row = lax.broadcasted_iota(jnp.int32, (LANE, LANE), 0)
    return row == lax.broadcasted_iota(jnp.int32, (LANE, LANE), 1)


class Halo:
    def __init__(self, src, rows_in, cols_out, cols_in, near, send, recv, at):
        gx, gy, m, n = at
        self.src, self.rows_in, self.cols_out, self.cols_in, self.near, self.at = src, rows_in, cols_out, cols_in, near, at
        self.size = size = src.shape[0] - 2 * ROW
        self.copies = []
        for i, (dx, dy) in enumerate(SIDES):
            side = 0 if max(dx, -1) > 0 or (dx == 0 and dy > 0) else 1
            if dx:
                source = src.at[pl.ds(*strip(dx, size, ROW, near)), pl.ds(*strip(dy, size, LANE, near))]
                target = rows_in.at[side, :, pl.ds(*strip(-dy, size, LANE, False))]
            else:
                source, target = cols_out.at[side], cols_in.at[side]
            self.copies.append(
                pltpu.make_async_remote_copy(
                    src_ref=source,
                    dst_ref=target,
                    send_sem=send.at[i],
                    recv_sem=recv.at[i],
                    device_id=(lax.rem(gx + dx + m, m), lax.rem(gy + dy + n, n)),
                    device_id_type=MESH,
                )
            )

    def start(self):
        self.pack()
        self.send()

    def pack(self):
        size, eye = self.size, diagonal()
        for side, dy in ((0, 1), (1, -1)):
            lane = (LANE + size - 1 if dy > 0 else LANE) if self.near else (LANE + size if dy > 0 else LANE - 1)
            tile = lane // LANE * LANE
            for b in range(size // LANE):
                block = self.src[ROW + b * LANE : ROW + (b + 1) * LANE, tile : tile + LANE]
                block = jnp.broadcast_to(block[:, lane - tile : lane - tile + 1], (LANE, LANE))
                self.cols_out[side, b : b + 1, :] = jnp.sum(jnp.where(eye, block, 0.0), axis=0, keepdims=True)

    def send(self):
        for c in self.copies:
            c.start()

    def wait(self):
        for c in self.copies:
            c.wait()

    def column(self, side):
        gx, gy, m, n = self.at
        inside = gy > 0 if side == 0 else gy < n - 1
        blocks = []
        for b in range(self.size // LANE):
            block = jnp.broadcast_to(self.cols_in[side, b : b + 1, :], (LANE, LANE))
            blocks.append(jnp.sum(jnp.where(diagonal(), block, 0.0), axis=1, keepdims=True))
        return jnp.where(inside, jnp.concatenate(blocks, axis=0), 0.0)

    def strips(self, side):
        gx, gy, m, n = self.at
        inside = gx > 0 if side == 0 else gx < m - 1
        value = jnp.where(inside, self.rows_in[side], 0.0)
        left, right = value[:, 0:LANE], value[:, LANE + self.size : 2 * LANE + self.size]
        return jnp.where(gy > 0, left, 0.0), value[:, LANE : LANE + self.size], jnp.where(gy < n - 1, right, 0.0)

    def surround(self, pad):
        size = self.size
        for side, start in ((0, 0), (1, ROW + size)):
            before, middle, after = self.strips(side)
            before = jnp.broadcast_to(before[:, LANE - 1 : LANE], (ROW, LANE))
            after = jnp.broadcast_to(after[:, 0:1], (ROW, LANE))
            pad[start : start + ROW, :] = jnp.concatenate([before, middle, after], axis=1)
        for side, start in ((0, 0), (1, LANE + size)):
            pad[ROW : ROW + size, start : start + LANE] = jnp.broadcast_to(self.column(side), (size, LANE))

    def fold(self, result):
        size = self.size
        first, last = slice(LANE, 2 * LANE), slice(size, size + LANE)
        for side, rows in ((0, slice(ROW, 2 * ROW)), (1, slice(size, size + ROW))):
            left, middle, right = self.strips(side)
            result[rows, LANE : LANE + size] += middle
            result[rows, first] += left
            result[rows, last] += right
        lane = lax.broadcasted_iota(jnp.int32, (size, LANE), 1)
        full = slice(ROW, ROW + size)
        result[full, first] += jnp.where(lane == 0, self.column(0), 0.0)
        result[full, last] += jnp.where(lane == LANE - 1, self.column(1), 0.0)


class Exchange:
    def __init__(self, src, dst, send, recv, at, slab, cols=None):
        self.src, self.dst, self.send, self.recv, self.at, self.slab = src, dst, send, recv, at, slab
        self.cols = slice(0, src.shape[1]) if cols is None else cols

    def rows(self, index):
        return pl.ds(pl.multiple_of(index * self.slab, self.slab), self.slab)

    def copy(self, k):
        gx, gy, m, n = self.at
        peer = lax.rem(gy + k, n)
        return pltpu.make_async_remote_copy(
            src_ref=self.src.at[self.rows(peer), self.cols],
            dst_ref=self.dst.at[self.rows(gy), self.cols],
            send_sem=self.send.at[k],
            recv_sem=self.recv.at[k],
            device_id=(gx, peer),
            device_id_type=MESH,
        )

    def own(self):
        here = self.rows(self.at[1])
        self.dst[here, self.cols] = self.src[here, self.cols]

    def start(self):
        @pl.loop(1, self.at[3])
        def _(k):
            self.copy(k).start()

        self.own()

    def wait(self):
        @pl.loop(1, self.at[3])
        def _(k):
            self.copy(k).wait()

    def start_ends(self):
        gy, n = self.at[1], self.at[3]
        self.own()
        for ends in (True, False):

            @pl.loop(1, n)
            def _(k):
                peer = lax.rem(gy + k, n)
                at_end = (peer == 0) | (peer == n - 1)

                @pl.when(at_end if ends else jnp.logical_not(at_end))
                def _():
                    self.copy(k).start()


def spread(ref):
    size = ref.shape[0]
    half = size // 2
    row = lax.broadcasted_iota(jnp.int32, (half, size), 0)
    col = lax.broadcasted_iota(jnp.int32, (half, size), 1)
    ref[0:half, :] = jnp.where(col == 2 * row, 1.0, 0.0).astype(jnp.bfloat16)
    ref[half:size, :] = jnp.where(col == 2 * row + 1, 1.0, 0.0).astype(jnp.bfloat16)


def refine(pad, wins, coef, rolled, high, low, size, rows):
    own = pad[:, LANE : LANE + size]
    lane = lax.broadcasted_iota(jnp.int32, own.shape, 1)
    for dj in (-1, 0, 1):
        value = own
        if dj:
            beyond = pad[:, 0:LANE] if dj < 0 else pad[:, LANE + size : 2 * LANE + size]
            beyond = jnp.concatenate([beyond] * (size // LANE), axis=1)
            value = jnp.where(lane == (0 if dj < 0 else size - 1), beyond, pltpu.roll(own, (-dj) % size, 1))
        rolled[...] = value
        for di in (-1, 0, 1):
            wins[3 * (di + 1) + dj + 1] = rolled[ROW + di : ROW + di + size, :]

    @pl.loop(0, size // rows)
    def _(step):
        at = pl.multiple_of(step * rows, rows)
        here = pl.ds(at, rows)
        totals = [None] * 4
        for near in range(9):
            window = wins[near, here, :]
            for child in range(4):
                term = coef[child, near, here, :].astype(jnp.float32) * window
                totals[child] = term if near == 0 else totals[child] + term
        for child in range(4):
            a, b = child // 2, child % 2
            there = pl.ds(pl.multiple_of(a * size + at, rows), rows)
            high[there, b * size : (b + 1) * size], low[there, b * size : (b + 1) * size] = split(totals[child])


def interleave(high, low, matrix, laced, size):
    for a in (0, 1):
        rows = slice(a * size, (a + 1) * size)
        value = f32dot(high[rows, :], matrix[...], (1, 0)) + f32dot(low[rows, :], matrix[...], (1, 0))
        for c in range(2 * size // LANE):
            laced[c, pl.ds(a, size, stride=2), :] = value[:, c * LANE : (c + 1) * LANE]


def parent_terms(quads, coef, shifted, result, size, rows):
    width = size + 2 * LANE
    tall = size + 4 * ROW
    for d in range(3):
        shifted[d, 0 : 2 * ROW, :] = jnp.zeros((2 * ROW, width), jnp.float32)
        shifted[d, tall - 2 * ROW : tall, :] = jnp.zeros((2 * ROW, width), jnp.float32)

    @pl.loop(0, size // rows)
    def _(step):
        at = pl.multiple_of(step * rows, rows)
        here = pl.ds(at, rows)
        quad = [
            quads[pl.ds(pl.multiple_of(a * size + at, rows), rows), b * size : (b + 1) * size]
            for a in (0, 1)
            for b in (0, 1)
        ]
        lane = lax.broadcasted_iota(jnp.int32, (rows, size), 1)
        for d in range(3):
            parts = []
            for j in range(3):
                part = None
                for child in range(4):
                    term = coef[child, 3 * d + j, here, :].astype(jnp.float32) * quad[child]
                    part = term if child == 0 else part + term
                parts.append(part if j == 1 else pltpu.roll(part, (j - 1) % size, 1))
            total = parts[1] + jnp.where(lane < size - 1, parts[0], 0.0) + jnp.where(lane > 0, parts[2], 0.0)
            before = jnp.where(lane == size - 1, parts[0], 0.0)[:, size - LANE : size]
            after = jnp.where(lane == 0, parts[2], 0.0)[:, 0:LANE]
            total = jnp.concatenate([before, total, after], axis=1)
            shifted[d, pl.ds(pl.multiple_of(at + 2 * ROW, ROW), rows), :] = total

    high = tall - 2 * ROW
    result[...] = (
        shifted[1, ROW : ROW + high, :]
        + shifted[2, ROW - 1 : ROW - 1 + high, :]
        + shifted[0, ROW + 1 : ROW + 1 + high, :]
    )


def rim_terms(quads, coef, shifted, result, size, rows):
    width = size + 2 * LANE
    tall = size + 4 * ROW
    for d in range(3):
        shifted[d, 0 : 2 * ROW, :] = jnp.zeros((2 * ROW, width), jnp.float32)
        shifted[d, tall - 2 * ROW : tall, :] = jnp.zeros((2 * ROW, width), jnp.float32)

    def term(near, at, start, length):
        here = pl.ds(at, rows)
        total = None
        for child in range(4):
            row = pl.ds(pl.multiple_of(child // 2 * size + at, rows), rows)
            column = child % 2 * size + start
            part = coef[child, near, here, start : start + length].astype(jnp.float32) * quads[row, column : column + length]
            total = part if child == 0 else total + part
        return total

    @pl.loop(0, size // rows)
    def _(step):
        at = pl.multiple_of(step * rows, rows)
        lane = lax.broadcasted_iota(jnp.int32, (rows, LANE), 1)
        for d in range(3):
            for j, start, edge, put in ((0, 0, 0, 0), (2, size - LANE, LANE - 1, LANE + size)):
                part = jnp.where(lane == edge, term(3 * d + j, at, start, LANE), 0.0)
                shifted[d, pl.ds(pl.multiple_of(at + 2 * ROW, ROW), rows), put : put + LANE] = pltpu.roll(
                    part, (j - 1) % LANE, 1
                )

    lane = lax.broadcasted_iota(jnp.int32, (rows, size), 1)
    for d, at in ((0, 0), (2, size - rows)):
        before = pltpu.roll(term(3 * d, at, 0, size), size - 1, 1)
        after = pltpu.roll(term(3 * d + 2, at, 0, size), 1, 1)
        total = term(3 * d + 1, at, 0, size) + jnp.where(lane < size - 1, before, 0.0) + jnp.where(lane > 0, after, 0.0)
        shifted[d, at + 2 * ROW : at + 2 * ROW + rows, LANE : LANE + size] = total

    def summed(start, length, cols):
        at = start + ROW
        return (
            shifted[1, at : at + length, cols]
            + shifted[2, at - 1 : at - 1 + length, cols]
            + shifted[0, at + 1 : at + 1 + length, cols]
        )

    for start in (0, ROW + size):
        result[start : start + ROW, :] = summed(start, ROW, slice(0, width))
    for start in (0, LANE + size):
        cols = slice(start, start + LANE)
        result[ROW : ROW + size, cols] = summed(ROW, size, cols)


def squares(x):
    return jnp.sum(x * x, axis=0, keepdims=True)


def fold_lanes(x):
    total = x[:, 0:LANE]
    for c in range(1, x.shape[1] // LANE):
        total = total + x[:, c * LANE : (c + 1) * LANE]
    return total


def kernel(
    m, n, cells,
    xi_c, xi_m, xi_f, co_m, co_f, k_u, k_v, v_d, f_t, f_w, f_c,
    g_c, g_m, g_f, pot,
    pad_c, pad_m, xm, xf, cm, cf, ku, kv, vd, kut,
    roll_c, roll_m, win_c, win_m, hi_c, lo_c, hi_m, lo_m, lace_c, lace_m, mat_c, mat_m,
    listed, weights, counts, total_s, meta, metas, mix_hi, mix_lo, sky, sky_2, edge, edges, late, lates, tiles, tiles_o, sums, fsum, damps, dsum, dslab, back_b, dsky, dtile, ends,
    quad_c, quad_m, shift_c, shift_m, res_c, res_m, res_r, grad_c, grad_m, grad_f, back_v,
    row_c, row_m, row_f, row_b, col_o, col_i,
    parts, part_y, part_x,
    load, few, save, sem_s, sem_r, a2a_s, a2a_r, sem_ls, sem_lr, sem_es, sem_er, sem_ts, sem_tr, sem_ys, sem_yr, sem_xs, sem_xr,
):
    gx, gy = lax.axis_index("gx"), lax.axis_index("gy")
    at = (gx, gy, m, n)
    nc, nm, nf = xi_c.shape[0], xi_m.shape[0], xi_f.shape[0]
    slab = nf // n
    facets = k_u.shape[1]
    bins = v_d.shape[2]

    barrier = pltpu.get_barrier_semaphore()
    greeted = 0
    for dx in (-1, 1):
        for dy in (-1, 1):
            pl.semaphore_signal(
                barrier, inc=1, device_id=(lax.rem(gx + dx + m, m), lax.rem(gy + dy + n, n)), device_id_type=MESH
            )
            greeted += 1
    for k in range(1, m):
        pl.semaphore_signal(barrier, inc=1, device_id=(lax.rem(gx + k, m), gy), device_id_type=MESH)
        greeted += 1
    for k in range(1, n):
        pl.semaphore_signal(barrier, inc=1, device_id=(gx, lax.rem(gy + k, n)), device_id_type=MESH)
        greeted += 1

    left, right, inside = slice(0, LANE), slice(nf - LANE, nf), slice(LANE, nf - LANE)
    halves = (slice(0, 2 * LANE), slice(2 * LANE, nf))
    moved = ((left, slice(0, LANE)), (right, slice(LANE, 2 * LANE)), (inside, halves[1]))
    small = [
        pltpu.make_async_copy(src, dst, few.at[i])
        for i, (src, dst) in enumerate(((f_t, listed), (f_w, weights), (f_c, counts)))
    ]
    loads = [
        pltpu.make_async_copy(src, dst, load.at[i])
        for i, (src, dst) in enumerate(
            (
                (xi_c, pad_c.at[ROW : ROW + nc, LANE : LANE + nc]),
                (co_m, cm),
                (xi_m, xm),
                (co_f, cf),
                (xi_f, xf),
                (k_u.at[0], ku),
                *((k_v.at[0, :, :, natural], kv.at[:, :, put]) for natural, put in moved),
                (v_d.at[0], vd),
            )
        )
    ]
    for c in loads[:3] + small + loads[3:]:
        c.start()

    def blank(pad, size):
        width = size + 2 * LANE
        pad[0:ROW, :] = jnp.zeros((ROW, width), jnp.float32)
        pad[ROW + size : 2 * ROW + size, :] = jnp.zeros((ROW, width), jnp.float32)
        pad[ROW : ROW + size, 0:LANE] = jnp.zeros((size, LANE), jnp.float32)
        pad[ROW : ROW + size, LANE + size : width] = jnp.zeros((size, LANE), jnp.float32)

    def middle_level():
        refine(pad_c, win_c, cm, roll_c, hi_c, lo_c, nc, 32)
        interleave(hi_c, lo_c, mat_c, lace_c, nc)
        for c in range(nm // LANE):
            cols = slice(c * LANE, (c + 1) * LANE)
            pad_m[ROW : ROW + nm, LANE + c * LANE : LANE + (c + 1) * LANE] = lace_c[c] + xm[:, cols]

    def fine_level(out):
        refine(pad_m, win_m, cf, roll_m, hi_m, lo_m, nm, 16)
        interleave(hi_m, lo_m, mat_m, lace_m, nm)
        for c in range(nf // LANE):
            cols = slice(c * LANE, (c + 1) * LANE)
            out[:, cols] = (lace_m[c] + xf[:, cols]).astype(jnp.bfloat16)

    def halo(i, src, rows_in, near):
        return Halo(src, rows_in, col_o.at[i], col_i.at[i], near, sem_s.at[i], sem_r.at[i], at)

    def exchange(i, src, dst, cols=None):
        return Exchange(src, dst, a2a_s.at[i], a2a_r.at[i], at, slab, cols)

    spread(mat_c)
    spread(mat_m)
    blank(pad_c, nc)
    blank(pad_m, nm)
    for c in small:
        c.wait()
    for f in range(facets):
        for s in range(2):
            i = 2 * f + s
            meta[i : i + 1, :] = jnp.full((1, LANE), listed[0, f, s].astype(jnp.float32))
            meta[4 + i : 5 + i, :] = jnp.full((1, LANE), weights[0, f, s])
    col_o[...] = jnp.zeros_like(col_o)
    loads[0].wait()
    halo_c = halo(0, pad_c, row_c, True)
    halo_c.pack()
    pl.semaphore_wait(barrier, greeted)
    halo_c.send()

    def meta_copy(k):
        return pltpu.make_async_remote_copy(
            src_ref=meta,
            dst_ref=metas.at[gy],
            send_sem=sem_ts.at[k],
            recv_sem=sem_tr.at[k],
            device_id=(gx, lax.rem(gy + k, n)),
            device_id_type=MESH,
        )

    @pl.loop(1, n)
    def _(k):
        meta_copy(k).start()

    metas[gy] = meta[...]
    for c in loads[1:3]:
        c.wait()
    middle_level()
    for c in loads[3:5]:
        c.wait()
    fine_level(sky)
    early = exchange(0, sky, tiles)

    halo_c.wait()
    halo_c.surround(pad_c)
    middle_level()
    halo_m = halo(1, pad_m, row_m, True)
    halo_m.start()
    early.start()

    @pl.loop(1, n)
    def _(k):
        meta_copy(k).wait()

    lane = lax.broadcasted_iota(jnp.int32, (slab, nf), 1)
    row = lax.broadcasted_iota(jnp.int32, (slab, nf), 0)
    tile_of = (lane // slab).astype(jnp.float32)
    same = lane % slab == row

    @pl.loop(0, n)
    def _(o):
        rows = pl.ds(pl.multiple_of(o * slab, slab), slab)
        value = metas[o]
        for f in range(facets):
            total = jnp.zeros((slab, nf), jnp.float32)
            for s in range(2):
                i = 2 * f + s
                tile = jnp.concatenate([value[i : i + 1, :]] * (nf // LANE), axis=1)
                weight = jnp.concatenate([value[4 + i : 5 + i, :]] * (nf // LANE), axis=1)
                total = total + jnp.where((tile == tile_of) & same, weight, 0.0)
            mix_hi[f, rows, :], mix_lo[f, rows, :] = split(total)

    owners = ((0, 0), (1, n - 1))

    def late_copy(e, owner, source):
        return pltpu.make_async_remote_copy(
            src_ref=late.at[e],
            dst_ref=lates.at[source],
            send_sem=sem_ls.at[e],
            recv_sem=sem_lr.at[source],
            device_id=(gx, owner),
            device_id_type=MESH,
        )

    halo_m.wait()
    halo_m.surround(pad_m)
    fine_level(sky_2)
    outer = lax.broadcasted_iota(jnp.int32, (nf, LANE), 1) < LANE // 2
    edge[...] = jnp.where(outer, sky_2[:, left], sky_2[:, right])
    rim = exchange(1, edge, edges)
    for e, owner in owners:
        start = owner * slab + e * (slab - END)
        rows = sky_2[start : start + END, :].astype(jnp.float32)[e * ROW : (e + 1) * ROW, :]
        late[e] = jnp.concatenate([rows[:, 0 : nf // 2], rows[:, nf // 2 : nf]], axis=0).astype(jnp.bfloat16)

        @pl.when(gy != owner)
        def _(e=e, owner=owner):
            late_copy(e, owner, gy).start()

        @pl.when(gy == owner)
        def _(e=e, owner=owner):
            lates[owner] = late[e]

    rim.start()

    prior = fold_lanes(squares(pad_c[ROW : ROW + nc, LANE : LANE + nc]))
    prior = prior + fold_lanes(squares(xm[...])) + fold_lanes(squares(xf[...]))
    parts[...] = jnp.zeros_like(parts)
    early.wait()
    for e, owner in owners:

        @pl.when(gy != owner)
        def _(e=e, owner=owner):
            late_copy(e, owner, gy).wait_send()

        @pl.when(gy == owner)
        def _(e=e, owner=owner):
            @pl.loop(1, n)
            def _(k):
                late_copy(e, owner, lax.rem(owner + k, n)).wait_recv()

            for i in range(n):
                at_row = i * slab + e * (slab - END)
                new = lates[i].astype(jnp.float32)
                new = jnp.concatenate([new[0:ROW, :], new[ROW : 2 * ROW, :]], axis=1)
                old = tiles[at_row : at_row + END, :].astype(jnp.float32)
                pair = [old[0:ROW, :], new] if e else [new, old[ROW:END, :]]
                tiles[at_row : at_row + END, :] = jnp.concatenate(pair, axis=0).astype(jnp.bfloat16)

    rim.wait()
    mixed = jnp.concatenate(
        [jnp.where(outer, edges[...], tiles[:, left]), jnp.where(outer, tiles[:, right], edges[...]), tiles[:, inside]],
        axis=1,
    )
    tiles_o[...] = mixed
    out = []
    for f in range(facets):
        sums[f] = (f32dot(mix_hi[f], tiles_o[...], (1, 0)) + f32dot(mix_lo[f], tiles_o[...], (1, 0))).astype(jnp.bfloat16)
        out.append(exchange(2 + f, sums.at[f], fsum.at[f]))
        out[f].start()

    for c in loads[5:]:
        c.wait()
    for f in range(facets):
        kut[f] = ku[f].T
    home = []
    chunk = 512
    for f in range(facets):
        out[f].wait()
        count = counts[0, f]

        for step in range(bins // chunk):
            here = slice(step * chunk, (step + 1) * chunk)
            amp = f32dot(ku[f, here, :], fsum[f], (1, 0)).astype(jnp.bfloat16)
            vis = f32dot(amp, kv[f], (1, 1))
            bin_at = step * chunk + lax.broadcasted_iota(jnp.int32, (chunk, bins), 0)
            resid = jnp.where(bin_at < count, vis - vd[f, here, :].astype(jnp.float32), 0.0)
            parts[...] += squares(resid)
            dvis = (inv_noise * resid).astype(jnp.bfloat16)
            damps[here, :] = f32dot(dvis, kv[f], (1, 0)).astype(jnp.bfloat16)

        for h, cols in enumerate(halves):
            dsum[f, :, cols] = f32dot(kut[f], damps[:, cols], (1, 0)).astype(jnp.bfloat16)
            going = exchange(2 + facets + 2 * f + h, dsum.at[f], dslab.at[f], cols)
            home.append(going)
            if f < facets - 1 or h == 0:
                going.start()
            else:
                going.start_ends()

    own = 0.5 * prior + 0.5 * inv_noise * fold_lanes(parts[...])
    part_y[gy] = jnp.where(lax.broadcasted_iota(jnp.int32, (ROW, LANE), 0) == 0, own, 0.0)

    def pot_y(k):
        return pltpu.make_async_remote_copy(
            src_ref=part_y.at[gy],
            dst_ref=part_y.at[gy],
            send_sem=sem_ys.at[k],
            recv_sem=sem_yr.at[k],
            device_id=(gx, lax.rem(gy + k, n)),
            device_id_type=MESH,
        )

    def pot_x(k):
        return pltpu.make_async_remote_copy(
            src_ref=part_x.at[gx],
            dst_ref=part_x.at[gx],
            send_sem=sem_xs.at[k],
            recv_sem=sem_xr.at[k],
            device_id=(lax.rem(gx + k, m), gy),
            device_id_type=MESH,
        )

    @pl.loop(1, n)
    def _(k):
        pot_y(k).start()

    def unmix(f, cols):
        return f32dot(mix_hi[f], dslab[f, :, cols], (0, 0))

    for f in range(facets - 1):
        for h, cols in enumerate(halves):
            home[2 * f + h].wait()
            part = unmix(f, cols)
            back_v[:, cols] = part if f == 0 else back_v[:, cols] + part
    def ends_copy(e, k):
        peer = lax.rem(gy + k, n)
        return pltpu.make_async_remote_copy(
            src_ref=back_b.at[ends_rows(e, peer), halves[1]],
            dst_ref=ends.at[e],
            send_sem=sem_es.at[e, k],
            recv_sem=sem_er.at[e, k],
            device_id=(gx, peer),
            device_id_type=MESH,
        )

    def ends_rows(e, index):
        return pl.ds(pl.multiple_of(index * slab + e * (slab - END), END), END)

    def ends_start():
        for e, owner in owners:

            @pl.when(gy == owner)
            def _(e=e):
                @pl.loop(1, n)
                def _(k):
                    ends_copy(e, k).start()

                ends[e] = back_b[ends_rows(e, gy), halves[1]]

    def ends_wait():
        for e, owner in owners:

            @pl.when(gy == owner)
            def _(e=e):
                @pl.loop(1, n)
                def _(k):
                    ends_copy(e, k).wait_send()

            @pl.when(gy != owner)
            def _(e=e, owner=owner):
                ends_copy(e, lax.rem(gy - owner + n, n)).wait_recv()

    last = []
    f = facets - 1
    for h, cols in enumerate(halves):
        home[2 * f + h].wait()
        part = unmix(f, cols)
        back_b[:, cols] = (back_v[:, cols] + part if f else part).astype(jnp.bfloat16)
        if h:
            ends_start()
        last.append(exchange(2 + 3 * facets + h, back_b, dsky, cols))
        last[h].start()

    @pl.loop(1, n)
    def _(k):
        pot_y(k).wait()

    part_x[gx] = jnp.sum(part_y[...], axis=0)

    @pl.loop(1, m)
    def _(k):
        pot_x(k).start()

    def adjoint_fine(terms, result):
        for a in (0, 1):
            rows = slice(a * nm, (a + 1) * nm)
            lined = f32dot(mat_m[rows, :], dtile[...], (1, 0)).astype(jnp.bfloat16)
            quad_m[rows, :] = f32dot(lined, mat_m[...], (1, 1))
        terms(quad_m, cf, shift_m, result, nm, 16)

    last[0].wait()
    dtile[:, left] = dsky[:, 0:LANE]
    dtile[:, right] = dsky[:, LANE : 2 * LANE]
    dtile[END : nf - END, inside] = jnp.zeros((nf - 2 * END, nf - 2 * LANE), jnp.bfloat16)
    ends_wait()
    dtile[0:END, inside] = ends[0]
    dtile[nf - END : nf, inside] = ends[1]
    adjoint_fine(rim_terms, res_r)
    halo_f = halo(2, res_r, row_f, False)
    halo_f.start()
    last[1].wait()
    dtile[:, inside] = dsky[:, halves[1]]
    adjoint_fine(parent_terms, res_m)
    grad_f[...] = dtile[...].astype(jnp.float32) + xf[...]
    save_f = pltpu.make_async_copy(grad_f, g_f, save.at[0])
    save_f.start()
    halo_f.wait()
    halo_f.fold(res_m)
    dmiddle = res_m[ROW : ROW + nm, LANE : LANE + nm]
    high, low = split(dmiddle)
    for a in (0, 1):
        rows = slice(a * nc, (a + 1) * nc)
        matrix = mat_c[rows, :]
        quad_c[rows, :] = f32dot(
            f32dot(matrix, high, (1, 0)).astype(jnp.bfloat16), mat_c[...], (1, 1)
        ) + f32dot(f32dot(matrix, low, (1, 0)).astype(jnp.bfloat16), mat_c[...], (1, 1))
    parent_terms(quad_c, cm, shift_c, res_c, nc, 32)
    halo_b = halo(3, res_c, row_b, False)
    halo_b.start()
    grad_m[...] = res_m[ROW : ROW + nm, LANE : LANE + nm] + xm[...]
    save_m = pltpu.make_async_copy(grad_m, g_m, save.at[1])
    save_m.start()

    @pl.loop(1, m)
    def _(k):
        pot_x(k).wait()

    total_s[0, 0] = jnp.sum(part_x[...]) / cells
    save_p = pltpu.make_async_copy(total_s, pot, save.at[3])
    save_p.start()
    halo_b.wait()
    halo_b.fold(res_c)
    grad_c[...] = res_c[ROW : ROW + nc, LANE : LANE + nc] + pad_c[ROW : ROW + nc, LANE : LANE + nc]
    save_c = pltpu.make_async_copy(grad_c, g_c, save.at[2])
    save_c.start()
    save_f.wait()
    save_m.wait()
    save_c.wait()
    save_p.wait()


def finish(*refs):
    count = (len(refs) - 2) // 3
    given, given_out, held = refs[:count], refs[count : 2 * count], refs[2 * count : 3 * count]
    come, go = refs[3 * count :]
    blocks = []
    for a, b, v in zip(given, given_out, held):
        rows = min(LANE, a.shape[0])
        for start in range(0, a.shape[0], rows):
            here = slice(start, start + rows)
            i = len(blocks)
            blocks.append(
                (
                    pltpu.make_async_copy(a.at[here, :], v.at[here, :], come.at[i]),
                    pltpu.make_async_copy(v.at[here, :], b.at[here, :], go.at[i]),
                )
            )
    for read, _ in blocks:
        read.start()
    for read, write in blocks:
        read.wait()
        write.start()
    for _, write in blocks:
        write.wait()


def body(
    xi_coarse, xi_middle, xi_fine, coef_middle, coef_fine, kern_u, kern_v, vis_data, facet_tiles, facet_weight, facet_count
):
    m, n = lax.axis_size("gx"), lax.axis_size("gy")
    nc, nm, nf = xi_coarse.shape[0], xi_middle.shape[0], xi_fine.shape[0]
    facets, bins = kern_u.shape[1], vis_data.shape[2]
    cells = float(m * n * nf * nf)
    f32, bf16 = jnp.float32, jnp.bfloat16
    vmem, dma = pltpu.VMEM, pltpu.SemaphoreType.DMA

    def wide(size):
        return vmem((size + 2 * ROW, size + 2 * LANE), f32)

    def strips(size):
        return vmem((2, ROW, size + 2 * LANE), f32)

    swaps = 4 + 3 * facets
    scratch = [
        wide(nc), wide(nm), vmem((nm, nm), f32), vmem((nf, nf), f32),
        vmem(coef_middle.shape, bf16), vmem(coef_fine.shape, bf16),
        vmem(kern_u.shape[1:], bf16), vmem(kern_v.shape[1:], bf16), vmem(vis_data.shape[1:], bf16),
        vmem((facets, nf, bins), bf16),
        vmem((nc + 2 * ROW, nc), f32), vmem((nm + 2 * ROW, nm), f32),
        vmem((9, nc, nc), f32), vmem((9, nm, nm), f32),
        vmem((nm, nm), bf16), vmem((nm, nm), bf16), vmem((nf, nf), bf16), vmem((nf, nf), bf16),
        vmem((nm // LANE, nm, LANE), f32), vmem((nf // LANE, nf, LANE), f32),
        vmem((nm, nm), bf16), vmem((nf, nf), bf16),
        pltpu.SMEM(facet_tiles.shape, jnp.int32), pltpu.SMEM(facet_weight.shape, f32),
        pltpu.SMEM(facet_count.shape, jnp.int32), pltpu.SMEM((1, 1), f32),
        vmem((8, LANE), f32), vmem((n, 8, LANE), f32), vmem((facets, nf, nf), bf16), vmem((facets, nf, nf), bf16),
        vmem((nf, nf), bf16), vmem((nf, nf), bf16), vmem((nf, LANE), bf16), vmem((nf, LANE), bf16),
        vmem((2, END, nf // 2), bf16), vmem((n, END, nf // 2), bf16), vmem((nf, nf), bf16), vmem((nf, nf), bf16),
        vmem((facets, nf, nf), bf16), vmem((facets, nf, nf), bf16),
        vmem((bins, nf), bf16), vmem((facets, nf, nf), bf16), vmem((facets, nf, nf), bf16),
        vmem((nf, nf), bf16), vmem((nf, nf), bf16), vmem((nf, nf), bf16), vmem((2, END, nf - 2 * LANE), bf16),
        vmem((nm, nm), f32), vmem((nf, nf), f32),
        vmem((3, nc + 4 * ROW, nc + 2 * LANE), f32), vmem((3, nm + 4 * ROW, nm + 2 * LANE), f32),
        wide(nc), wide(nm), wide(nm), vmem((nc, nc), f32), vmem((nm, nm), f32), vmem((nf, nf), f32), vmem((nf, nf), f32),
        strips(nc), strips(nm), strips(nm), strips(nc), vmem((4, 2, ROW, LANE), f32), vmem((4, 2, ROW, LANE), f32),
        vmem((1, bins), f32), vmem((n, 8, LANE), f32), vmem((m, 8, LANE), f32),
        dma((10,)), dma((3,)), dma((4,)), dma((4, 8)), dma((4, 8)),
        dma((swaps, n)), dma((swaps, n)), dma((2,)), dma((n,)), dma((2, n)), dma((2, n)),
        dma((n,)), dma((n,)), dma((n,)), dma((n,)), dma((m,)), dma((m,)),
    ]
    hbm = pl.BlockSpec(memory_space=pl.ANY)
    shapes = [jax.ShapeDtypeStruct(x.shape, f32) for x in (xi_coarse, xi_middle, xi_fine)]
    *grads, total = pl.pallas_call(
        functools.partial(kernel, m, n, cells),
        name="prior_gradient",
        out_shape=(*shapes, jax.ShapeDtypeStruct((1, 1), f32)),
        in_specs=[hbm] * 11,
        out_specs=[hbm] * 4,
        scratch_shapes=scratch,
        compiler_params=pltpu.CompilerParams(
            collective_id=0, has_side_effects=True, vmem_limit_bytes=62 * 1024 * 1024
        ),
    )(
        xi_coarse, xi_middle, xi_fine, coef_middle, coef_fine, kern_u, kern_v, vis_data,
        facet_tiles, facet_weight, facet_count,
    )
    grads = pl.pallas_call(
        finish,
        name="hand_out",
        out_shape=shapes,
        in_specs=[hbm] * 3,
        out_specs=[hbm] * 3,
        scratch_shapes=[*[vmem(s.shape, f32) for s in shapes], dma((8,)), dma((8,))],
    )(*grads)
    return (*grads, total.reshape(()))


def solution(mesh):
    placed = (
        P("gx", "gy"),
        P("gx", "gy"),
        P("gx", "gy"),
        P(None, None, "gx", "gy"),
        P(None, None, "gx", "gy"),
        P("gx", "gy", None, None),
        P("gx", "gy", None, None),
        P("gx", "gy", None, None),
        P("gx", "gy", None),
        P("gx", "gy", None),
        P("gx", "gy"),
    )
    return jax.shard_map(
        body,
        mesh=mesh,
        in_specs=placed,
        out_specs=(P("gx", "gy"), P("gx", "gy"), P("gx", "gy"), P()),
        check_vma=False,
    )
```
